32 devices in a mesh: blk: 4 (over y, x), rep: 8 (over z, core).
Axes of the slice: x: 2, y: 2, z: 4, core: 2. Of those that a mesh axis runs over, the one named last changes fastest.
Arguments:
- query_hidden: bfloat16 [8, 16, 32, 768], P('rep', 'blk'), may hold values from -18 to 18
- passage_hidden: bfloat16 [8, 16, 512, 768], P('rep', 'blk'), may hold values from -6 to 6
- lengths: int32 [8, 16], P('rep', 'blk'), may hold values from 64 to 512
- projection: bfloat16 [768, 128], replicated, may hold values from -0.21875 to 0.21875
Outputs:
- query_grad: float32 [8, 16, 32, 128], P('rep', 'blk')
- passage_grad: float32 [8, 16, 512, 128], P('rep', 'blk')
- grad_weight: float32 [768, 128], replicated
- loss: float32 [], replicated
The draws below stay inside these ranges and needn't reach their ends.
All inputs are finite; a program needn't handle non-finite values.
Results may differ from the reference program's by a relative error of at most 0.0097.
Values may be sent and summed in bfloat16 or wider, within the bound.
A program may use at most 128 MiB of HBM per device.

```python
import jax
import jax.numpy as jnp
from jax import lax

H = 768
DIM = 128
QLEN = 32
PLEN = 512
QN = 16
PN = 16
NQ_ALL = 128
N_REP = 8


def shared_passages(key):
    noise = jax.random.normal(jax.random.fold_in(key, 11), (N_REP, PN, PLEN, H), jnp.float32)
    values = jnp.clip(noise, -6.0, 6.0)
    return values


def draw_passage_hidden(key, part):
    return shared_passages(key).astype(jnp.bfloat16)


def draw_query_hidden(key, part):
    noise = jax.random.normal(jax.random.fold_in(key, 13), (N_REP, QN, QLEN, H), jnp.float32)
    values = 0.1 * jnp.clip(noise, -6.0, 6.0)
    return values.astype(jnp.bfloat16)


def touch_ends(values, stream_key, least, top_value):
    dims = values.shape
    spot = [jax.random.randint(jax.random.fold_in(stream_key, axis), (), 0, dims[axis]) for axis in range(len(dims))]
    values = values.at[tuple(spot)].set(least)
    longest = dims.index(max(dims))
    spot[longest] = (spot[longest] + 1) % dims[longest]
    return values.at[tuple(spot)].set(top_value)


def bell_draw(key, extent, width, reach, kind=jnp.bfloat16):
    values = jax.random.normal(key, extent, jnp.float32) * width
    return jnp.minimum(jnp.maximum(values, -reach), reach).astype(kind)


def setup_inputs(seed: int = 0) -> dict:
    key_list = jax.random.split(jax.random.key(seed), 5)
    query_hidden = draw_query_hidden(jax.random.fold_in(key_list[4], 71), 0)
    passage_hidden = draw_passage_hidden(jax.random.fold_in(key_list[4], 71), 0)
    lengths = touch_ends(jax.random.randint(key_list[2], (N_REP, PN), PLEN // 8, PLEN + 1), jax.random.fold_in(key_list[2], 1), PLEN // 8, PLEN).astype(jnp.int32)
    projection = bell_draw(key_list[3], (H, DIM), H ** -0.5, 0.21875)
    return dict(query_hidden=query_hidden, passage_hidden=passage_hidden, lengths=lengths, projection=projection)


temper = 0.5


def soft_scores(scores, lens):
    slots = scores.shape[-1]
    valid = lax.broadcasted_iota(jnp.int32, (lens.shape[0], slots), 1) < lens[:, None]
    scaled = jnp.where(valid[None], scores / temper, -jnp.inf)
    top = jnp.max(scaled, -1, keepdims=True)
    logz = top + jnp.log(jnp.sum(jnp.exp(scaled - top), -1, keepdims=True))
    pooled = temper * (logz[..., 0] - jnp.log(lens.astype(jnp.float32))[None])
    return pooled, scaled, logz


def group_step(inputs):
    qhid, phid, lens, projection = inputs
    hidden = projection.shape[0]
    qtok = jnp.dot(qhid.reshape(-1, hidden), projection, preferred_element_type=jnp.float32).astype(jnp.bfloat16)
    ptok = jnp.dot(phid.reshape(-1, hidden), projection, preferred_element_type=jnp.float32).astype(jnp.bfloat16)
    nquery = qhid.shape[0]
    qlen = qhid.shape[1]
    npass = phid.shape[0]
    plen = phid.shape[1]
    scores = jnp.dot(qtok, ptok.T, preferred_element_type=jnp.float32).reshape(nquery * qlen, npass, plen)
    pooled, scaled, logz = soft_scores(scores, lens)
    score = jnp.sum(pooled.reshape(nquery, qlen, npass), 1)
    top = jnp.max(score, 1, keepdims=True)
    lse = top + jnp.log(jnp.sum(jnp.exp(score - top), 1, keepdims=True))
    target = lax.broadcasted_iota(jnp.int32, score.shape, 1) == lax.broadcasted_iota(jnp.int32, score.shape, 0)
    loss_part = jnp.sum(lse[:, 0] - jnp.sum(jnp.where(target, score, 0.0), 1))
    dscore = (jnp.exp(score - lse) - target.astype(jnp.float32)) / NQ_ALL
    spread = jnp.repeat(dscore, qlen, axis=0)
    grad_a = (spread[:, :, None] * jnp.exp(scaled - logz)).astype(jnp.bfloat16).reshape(nquery * qlen, npass * plen)
    qgrad = jnp.dot(grad_a, ptok, preferred_element_type=jnp.float32)
    pgrad = jnp.dot(grad_a.T, qtok, preferred_element_type=jnp.float32)
    wgrad = jnp.dot(qhid.reshape(-1, hidden).T, qgrad.astype(jnp.bfloat16), preferred_element_type=jnp.float32)
    wgrad = wgrad + jnp.dot(phid.reshape(-1, hidden).T, pgrad.astype(jnp.bfloat16), preferred_element_type=jnp.float32)
    return qgrad.reshape(nquery, qlen, -1), pgrad.reshape(npass, plen, -1), wgrad, loss_part


def reference(query_hidden, passage_hidden, lengths, projection):
    copies = jnp.broadcast_to(projection, (query_hidden.shape[0],) + projection.shape)
    qgrad, pgrad, wgrad, losses = lax.map(group_step, (query_hidden, passage_hidden, lengths, copies))
    return qgrad, pgrad, jnp.sum(wgrad, 0), jnp.sum(losses) / NQ_ALL
```

```python
import functools

import jax
import jax.numpy as jnp
from jax import lax
from jax.experimental import pallas as pl
from jax.experimental.pallas import tpu as pltpu
from jax.sharding import PartitionSpec as P

MESH = pl.DeviceIdType.MESH
F32 = jnp.float32
BF16 = jnp.bfloat16
NT = (((1,), (1,)), ((), ()))

temper = 0.5
LANES = 128
LOG2E = 1.4426950408889634
FAR = -1e30


def rows_iota(shape, dim):
    return lax.broadcasted_iota(jnp.int32, shape, dim)


def split_dot(x, ones, terms):
    out = None
    for _ in range(terms):
        part = x.astype(BF16)
        x = x - part.astype(F32)
        dot = jnp.dot(part, ones, preferred_element_type=F32)
        out = dot if out is None else out + dot
    return out


def kernel(
    dims, lens_in, qhid_in, proj_in, phid, qg_out, pg_v, wg_out, loss_out,
    lens, proj, pick, spread, tok, ptok, ptok_t, hid, expo, reach, grads, tops, sums, sc, lo_c, lo_z, qsend, qrecv,
    wsend, wrecv, zbuf, cbuf,
    in_sem, up, down, tok_s, tok_r, hid_s, hid_r, sc_s, sc_r, lc_s, lc_r, lz_s, lz_r, qg_s, qg_r, ws_s, ws_r,
    z_s, z_r, c_s, c_r,
):
    nblk, nrep, ncore, nquery, qlen, npass, plen = dims
    ntok = nquery * qlen
    nqi = nblk * ntok
    nq_all = nblk * nquery
    ntp = npass * plen
    nz = nrep // ncore
    na = nblk * ncore
    hidden, dim = proj.shape
    total = nq_all * nrep
    parts = wsend.shape[0]
    cols = hidden // parts
    paired = nblk & (nblk - 1) == 0
    blk = lax.axis_index("blk")
    rep = lax.axis_index("rep")
    core = lax.rem(rep, ncore)
    zed = rep // ncore
    me_a = blk * ncore + core

    def blk_at(k):
        if not paired:
            return lax.rem(blk + k, nblk)
        out = 0
        bit = 1
        while bit < nblk:
            out = out + lax.rem(blk // bit + k // bit, 2) * bit
            bit *= 2
        return out

    def slot_owner(slots):
        return slots ^ blk if paired else lax.rem(blk + nblk - slots, nblk)

    def blk_peer(k):
        return (blk_at(k), rep)

    def core_peer(k):
        return (blk, zed * ncore + lax.rem(core + k, ncore))

    def a_index(k):
        return lax.rem(me_a + k, na)

    def a_peer(k):
        other = a_index(k)
        return (other // ncore, zed * ncore + lax.rem(other, ncore))

    def z_peer(k):
        return (blk, lax.rem(zed + k, nz) * ncore + core)

    def z_next(step):
        return (blk, (zed + step) * ncore + core)

    def share(src, dst, send, recv, peer, count):
        copies = []
        for k in range(1, count):
            copy = pltpu.make_async_remote_copy(
                src_ref=src(k), dst_ref=dst(k), send_sem=send.at[k - 1], recv_sem=recv.at[k - 1],
                device_id=peer(k), device_id_type=MESH,
            )
            copy.start()
            copies.append(copy)
        return copies

    def tell(step):
        @pl.when((zed >= step) & (zed + 1 < nz))
        def _():
            pl.semaphore_signal(up.at[step - 1], inc=1, device_id=z_next(1), device_id_type=MESH)

        @pl.when((zed + step < nz) & (zed >= 1))
        def _():
            pl.semaphore_signal(down.at[step - 1], inc=1, device_id=z_next(-1), device_id_type=MESH)

    def hear(step):
        @pl.when(zed >= step + 1)
        def _():
            pl.semaphore_wait(up.at[step - 1], 1)

        @pl.when(zed + step + 1 < nz)
        def _():
            pl.semaphore_wait(down.at[step - 1], 1)

    barrier = pltpu.get_barrier_semaphore()
    for k in range(1, na):
        pl.semaphore_signal(barrier, inc=1, device_id=a_peer(k), device_id_type=MESH)

    @pl.when(zed + 1 < nz)
    def _():
        pl.semaphore_signal(barrier, inc=1, device_id=z_next(1), device_id_type=MESH)

    @pl.when(zed >= 1)
    def _():
        pl.semaphore_signal(barrier, inc=1, device_id=z_next(-1), device_id_type=MESH)

    greeted = na - 1 + (zed + nz - 1) // nz + (2 * nz - 2 - zed) // nz

    loads = []
    pairs = [(qhid_in, hid.at[pl.ds(ntp, ntok)]), (proj_in, proj), (lens_in, lens)]
    pairs += [(phid.at[p], hid.at[pl.ds(p * plen, plen)]) for p in range(npass)]
    for n, (src, dst) in enumerate(pairs):
        load = pltpu.make_async_copy(src, dst, in_sem.at[n])
        load.start()
        loads.append(load)
    ppad, qpad = sc.shape[1:]
    token = rows_iota((nqi, qpad), 0)
    query = slot_owner(token // ntok) * nquery + lax.rem(token, ntok) // qlen
    pick[...] = jnp.where(query == rows_iota((nqi, qpad), 1), 1.0, 0.0).astype(BF16)
    token_t = rows_iota((qpad, nqi), 1)
    query_t = slot_owner(token_t // ntok) * nquery + lax.rem(token_t, ntok) // qlen
    spread[...] = jnp.where(query_t == rows_iota((qpad, nqi), 0), 1.0, 0.0).astype(BF16)
    tops[...] = jnp.zeros_like(tops)
    sums[...] = jnp.ones_like(sums)
    unit = jnp.where(rows_iota((ntok, LANES), 1) == 0, 1.0, 0.0).astype(BF16)
    loads[0].wait()
    loads[1].wait()
    tok[0] = jnp.dot(hid[ntp : ntp + ntok, :], proj[...], preferred_element_type=F32).astype(BF16)
    pl.semaphore_wait(barrier, greeted)
    tok_copies = share(lambda k: tok.at[0], lambda k: tok.at[k], tok_s, tok_r, blk_peer, nblk)
    hid_copies = share(
        lambda k: qhid_in, lambda k: hid.at[pl.ds(ntp + k * ntok, ntok)], hid_s, hid_r, blk_peer, nblk
    )
    if nz > 2:
        tell(1)

    loads[2].wait()
    size = jnp.ones((ppad, LANES), jnp.int32)
    for p in range(npass):
        loads[3 + p].wait()
        vec = jnp.dot(hid[p * plen : (p + 1) * plen, :], proj[...], preferred_element_type=F32).astype(BF16)
        ptok[p, :, :dim] = vec
        out_of = (rows_iota((plen, LANES), 0) >= lens[0, p]) & (rows_iota((plen, LANES), 1) == 0)
        ptok[p, :, dim:] = jnp.where(out_of, FAR, 0.0).astype(BF16)
        ptok_t[p] = vec.T
        size = jnp.where(rows_iota((ppad, LANES), 0) == p, lens[0, p], size)

    def forward(first, count):
        width = count * ntok
        side = jnp.concatenate([tok[k] for k in range(first, first + count)], 0)
        side = jnp.concatenate([side, jnp.concatenate([unit] * count, 0)], 1)
        here = pl.ds(first * ntok, width)
        for p in range(npass):
            a = lax.dot_general(ptok[p], side, NT, preferred_element_type=F32)
            top = jnp.max(a, 0, keepdims=True)
            e = jnp.exp2((a - top) * (LOG2E / temper))
            expo[p, :, here] = e.astype(BF16)
            tops[pl.ds(p, 1), here] = top
            sums[pl.ds(p, 1), here] = jnp.sum(e, 0, keepdims=True)

    forward(0, 1)
    for k in range(1, nblk - 1):
        tok_copies[k - 1].wait_recv()
    if nblk > 2:
        forward(1, nblk - 2)
    if nblk > 1:
        tok_copies[nblk - 2].wait_recv()
        forward(nblk - 1, 1)

    log_size = jnp.log(size.astype(F32))[:, :1]
    pooled = temper * (tops[...] * (1.0 / temper) + jnp.log(sums[...]) - log_size)
    own = split_dot(pooled, pick[...], 3)
    sc[0] = own
    sc_copies = share(lambda k: sc.at[0], lambda k: sc.at[k], sc_s, sc_r, blk_peer, nblk)
    inv = 1.0 / sums[...]
    every_t = jnp.concatenate([tok[k].astype(F32).T for k in range(nblk)], 1)
    for p in range(npass):
        reach[p] = jnp.dot(ptok_t[p], expo[p], preferred_element_type=F32)
    if nz > 2:
        for step in range(1, nz - 1):
            hear(step)
            if step + 1 < nz - 1:
                tell(step + 1)
    for copy in sc_copies:
        copy.wait_recv()

    score = sc[...]
    row = rows_iota(score.shape, 1)
    lane = rows_iota(score.shape, 2)
    slot = rows_iota(score.shape, 0)
    live = row < npass
    hidden_score = jnp.where(live, score, -jnp.inf)
    top = jnp.max(jnp.max(hidden_score, 0), 0, keepdims=True)
    lse = top + jnp.log(jnp.sum(jnp.sum(jnp.exp(hidden_score - top[None]), 0), 0, keepdims=True))
    mine = rows_iota(own.shape, 0) + blk * npass == rows_iota(own.shape, 1)
    dscore = (jnp.exp(sc[0] - lse) - mine.astype(F32)) / total
    factor = split_dot(dscore, spread[...], 3) * inv

    qg_t = reach[0] * factor[0:1]
    for p in range(1, npass):
        qg_t = qg_t + reach[p] * factor[p : p + 1]
    qg_b = qg_t.astype(BF16)
    grads[:, ntp:] = qg_b
    for k in range(1, nblk):
        qsend[k] = qg_b[:, k * ntok : (k + 1) * ntok]
    qg_copies = share(lambda k: qsend.at[k], lambda k: qrecv.at[k], qg_s, qg_r, blk_peer, nblk)

    for p in range(npass):
        side = (every_t * factor[p : p + 1]).astype(BF16)
        g = lax.dot_general(expo[p], side, NT, preferred_element_type=F32)
        pg_v[p] = g
        grads[:, p * plen : (p + 1) * plen] = g.astype(BF16).T

    hit = live & (slot_owner(slot) * npass + row == lane)
    aim = jnp.sum(jnp.sum(jnp.where(hit, score, 0.0), 0), 0, keepdims=True)
    gap = jnp.where(rows_iota(lse.shape, 1) < nq_all, lse - aim, 0.0)
    lo_c[core] = jnp.broadcast_to(jnp.sum(gap, 1, keepdims=True), lo_c.shape[1:])
    lc_copies = share(lambda k: lo_c.at[core], lambda k: lo_c.at[core], lc_s, lc_r, core_peer, ncore)

    for copy in hid_copies:
        copy.wait_recv()
    ws_copies = []
    for h in range(parts):
        w = jnp.dot(grads[...], hid[:, h * cols : (h + 1) * cols], preferred_element_type=F32)
        w = w.T.astype(BF16).reshape(na, cols // na, dim)
        wsend[h] = w
        wrecv[h, me_a] = wsend[h, me_a]
        ws_copies.append(share(
            lambda k: wsend.at[h, a_index(k)], lambda k: wrecv.at[h, me_a], ws_s.at[h], ws_r.at[h], a_peer, na
        ))

    for copy in lc_copies:
        copy.wait_recv()
    lo_z[zed] = jnp.sum(lo_c[...], 0)
    lz_copies = share(lambda k: lo_z.at[zed], lambda k: lo_z.at[zed], lz_s, lz_r, z_peer, nz)
    for copy in qg_copies:
        copy.wait_recv()
    mine_t = grads[:, ntp : ntp + ntok].astype(F32)
    for k in range(1, nblk):
        mine_t = mine_t + qrecv[k].astype(F32)
    qg_out[...] = mine_t.T

    z_copies = []
    for h in range(parts):
        for copy in ws_copies[h]:
            copy.wait_recv()
        zbuf[h, zed] = jnp.sum(wrecv[h].astype(F32), 0).astype(BF16)
        z_copies.append(share(
            lambda k: zbuf.at[h, zed], lambda k: zbuf.at[h, zed], z_s.at[h], z_r.at[h], z_peer, nz
        ))
    for copy in lz_copies:
        copy.wait_recv()
    loss_out[...] = jnp.sum(lo_z[...], 0) / total
    c_copies = []
    for h in range(parts):
        for copy in z_copies[h]:
            copy.wait_recv()
        cbuf[h, me_a] = jnp.sum(zbuf[h].astype(F32), 0).astype(BF16)
        c_copies.append(share(
            lambda k: cbuf.at[h, me_a], lambda k: cbuf.at[h, me_a], c_s.at[h], c_r.at[h], a_peer, na
        ))
    for copy in tok_copies + hid_copies + sc_copies + qg_copies + lc_copies + lz_copies:
        copy.wait_send()
    for h in range(parts):
        for copy in ws_copies[h] + z_copies[h]:
            copy.wait_send()
    for h in range(parts):
        for copy in c_copies[h]:
            copy.wait_recv()
        wg_out[h * cols : (h + 1) * cols, :] = cbuf[h].astype(F32).reshape(cols, dim)
    for h in range(parts):
        for copy in c_copies[h]:
            copy.wait_send()


def write_out(qg, pg, wg, loss, qg_out, pg_out, wg_out, loss_out, sem):
    copies = []
    for n, (src, dst) in enumerate(((pg, pg_out), (wg, wg_out), (qg, qg_out))):
        copy = pltpu.make_async_copy(src, dst, sem.at[n])
        copy.start()
        copies.append(copy)
    loss_out[0, 0] = loss[0, 0]
    for copy in copies:
        copy.wait()


def shards(query_hidden, passage_hidden, lengths, projection):
    hidden, dim = projection.shape
    nquery, qlen = query_hidden.shape[1:3]
    npass, plen = passage_hidden.shape[1:3]
    nblk = lax.axis_size("blk")
    nrep = lax.axis_size("rep")
    ncore = 2 if nrep % 2 == 0 else 1
    nz = nrep // ncore
    na = nblk * ncore
    ntok = nquery * qlen
    nqi = nblk * ntok
    ntp = npass * plen
    ppad = -(-npass // 8) * 8
    qpad = -(-nblk * nquery // LANES) * LANES
    parts = 3 if hidden % (3 * 16 * na) == 0 else 1
    deep = hidden // parts // na
    dims = (nblk, nrep, ncore, nquery, qlen, npass, plen)
    vmem = pl.BlockSpec(memory_space=pltpu.VMEM)
    sem = lambda *n: pltpu.SemaphoreType.DMA(tuple(max(i, 1) for i in n))
    flag = pltpu.SemaphoreType.REGULAR((max(nz - 2, 1),))
    pairs = []
    for n in (nblk, nblk, nblk, ncore, nz, nblk):
        pairs += [sem(n - 1), sem(n - 1)]
    for n in (na, nz, na):
        pairs += [sem(parts, n - 1), sem(parts, n - 1)]
    held = pl.pallas_call(
        functools.partial(kernel, dims),
        out_shape=(
            pltpu.VMEM((ntok, dim), F32),
            pltpu.VMEM((npass, plen, dim), F32),
            pltpu.VMEM((hidden, dim), F32),
            pltpu.VMEM((8, LANES), F32),
        ),
        in_specs=[
            *[pl.BlockSpec(memory_space=pl.ANY)] * 4,
        ],
        out_specs=(vmem, vmem, vmem, vmem),
        scratch_shapes=[
            pltpu.SMEM((1, npass), jnp.int32),
            pltpu.VMEM((hidden, dim), BF16),
            pltpu.VMEM((nqi, qpad), BF16),
            pltpu.VMEM((qpad, nqi), BF16),
            pltpu.VMEM((nblk, ntok, dim), BF16),
            pltpu.VMEM((npass, plen, dim + LANES), BF16),
            pltpu.VMEM((npass, dim, plen), BF16),
            pltpu.VMEM((ntp + nqi, hidden), BF16),
            pltpu.VMEM((npass, plen, nqi), BF16),
            pltpu.VMEM((npass, dim, nqi), F32),
            pltpu.VMEM((dim, ntp + nqi), BF16),
            pltpu.VMEM((ppad, nqi), F32),
            pltpu.VMEM((ppad, nqi), F32),
            pltpu.VMEM((nblk, ppad, qpad), F32),
            pltpu.VMEM((ncore, 8, LANES), F32),
            pltpu.VMEM((nz, 8, LANES), F32),
            pltpu.VMEM((nblk, dim, ntok), BF16),
            pltpu.VMEM((nblk, dim, ntok), BF16),
            pltpu.VMEM((parts, na, deep, dim), BF16),
            pltpu.VMEM((parts, na, deep, dim), BF16),
            pltpu.VMEM((parts, nz, deep, dim), BF16),
            pltpu.VMEM((parts, na, deep, dim), BF16),
            sem(npass + 3),
            flag,
            flag,
        ] + pairs,
        compiler_params=pltpu.CompilerParams(
            collective_id=0, has_side_effects=True, vmem_limit_bytes=56 << 20
        ),
    )(
        lengths,
        query_hidden.reshape(ntok, hidden),
        projection,
        passage_hidden.reshape(npass, plen, hidden),
    )
    hbm = pl.BlockSpec(memory_space=pl.ANY)
    qg, pg, wg, loss = pl.pallas_call(
        write_out,
        out_shape=(
            jax.ShapeDtypeStruct((ntok, dim), F32),
            jax.ShapeDtypeStruct((npass, plen, dim), F32),
            jax.ShapeDtypeStruct((hidden, dim), F32),
            jax.ShapeDtypeStruct((1, 1), F32),
        ),
        in_specs=[vmem] * 4,
        out_specs=(hbm, hbm, hbm, pl.BlockSpec(memory_space=pltpu.SMEM)),
        scratch_shapes=[sem(3)],
        compiler_params=pltpu.CompilerParams(vmem_limit_bytes=8 << 20),
    )(*[pltpu.with_memory_space_constraint(x, pltpu.VMEM) for x in held])
    return (
        qg.reshape(1, nquery, qlen, dim),
        pg.reshape(1, npass, plen, dim),
        wg,
        loss.reshape(()),
    )


def solution(mesh):
    return jax.shard_map(
        shards,
        mesh=mesh,
        in_specs=(P("rep", "blk", None, None), P("rep", "blk", None, None), P("rep", "blk"), P()),
        out_specs=(P("rep", "blk", None, None), P("rep", "blk", None, None), P(), P()),
        check_vma=False,
    )
```

```python
import functools

import jax
import jax.numpy as jnp
from jax import lax
from jax.experimental import pallas as pl
from jax.experimental.pallas import tpu as pltpu
from jax.sharding import PartitionSpec as P

MESH = pl.DeviceIdType.MESH
F32 = jnp.float32
BF16 = jnp.bfloat16
NT = (((1,), (1,)), ((), ()))

temper = 0.5
LANES = 128
LOG2E = 1.4426950408889634
FAR = -1e30


def rows_iota(shape, dim):
    return lax.broadcasted_iota(jnp.int32, shape, dim)


def split_dot(x, ones, terms):
    out = None
    for _ in range(terms):
        part = x.astype(BF16)
        x = x - part.astype(F32)
        dot = jnp.dot(part, ones, preferred_element_type=F32)
        out = dot if out is None else out + dot
    return out


def kernel(
    dims, lens_in, qhid_in, proj_in, phid, qg_out, pg_v, wg_out, loss_out,
    lens, proj, pick, spread, tok, ptok, ptok_t, hid, expo, reach, grads, tops, sums, sc, lo_c, lo_z, qsend, qrecv,
    wsend, wrecv, zbuf, cbuf,
    in_sem, up, down, tok_s, tok_r, hid_s, hid_r, sc_s, sc_r, lc_s, lc_r, lz_s, lz_r, qg_s, qg_r, ws_s, ws_r,
    z_s, z_r, c_s, c_r,
):
    nblk, nrep, ncore, nquery, qlen, npass, plen = dims
    ntok = nquery * qlen
    nqi = nblk * ntok
    nq_all = nblk * nquery
    ntp = npass * plen
    nz = nrep // ncore
    na = nblk * ncore
    hidden, dim = proj.shape
    total = nq_all * nrep
    parts = wsend.shape[0]
    cols = hidden // parts
    paired = nblk & (nblk - 1) == 0
    blk = lax.axis_index("blk")
    rep = lax.axis_index("rep")
    core = lax.rem(rep, ncore)
    zed = rep // ncore
    me_a = blk * ncore + core

    def blk_at(k):
        if not paired:
            return lax.rem(blk + k, nblk)
        out = 0
        bit = 1
        while bit < nblk:
            out = out + lax.rem(blk // bit + k // bit, 2) * bit
            bit *= 2
        return out

    def slot_owner(slots):
        return slots ^ blk if paired else lax.rem(blk + nblk - slots, nblk)

    def blk_peer(k):
        return (blk_at(k), rep)

    def core_peer(k):
        return (blk, zed * ncore + lax.rem(core + k, ncore))

    def a_index(k):
        return lax.rem(me_a + k, na)

    def a_peer(k):
        other = a_index(k)
        return (other // ncore, zed * ncore + lax.rem(other, ncore))

    def z_peer(k):
        return (blk, lax.rem(zed + k, nz) * ncore + core)

    def z_next(step):
        return (blk, (zed + step) * ncore + core)

    def share(src, dst, send, recv, peer, count):
        copies = []
        for k in range(1, count):
            copy = pltpu.make_async_remote_copy(
                src_ref=src(k), dst_ref=dst(k), send_sem=send.at[k - 1], recv_sem=recv.at[k - 1],
                device_id=peer(k), device_id_type=MESH,
            )
            copy.start()
            copies.append(copy)
        return copies

    def tell(step):
        @pl.when((zed >= step) & (zed + 1 < nz))
        def _():
            pl.semaphore_signal(up.at[step - 1], inc=1, device_id=z_next(1), device_id_type=MESH)

        @pl.when((zed + step < nz) & (zed >= 1))
        def _():
            pl.semaphore_signal(down.at[step - 1], inc=1, device_id=z_next(-1), device_id_type=MESH)

    def hear(step):
        @pl.when(zed >= step + 1)
        def _():
            pl.semaphore_wait(up.at[step - 1], 1)

        @pl.when(zed + step + 1 < nz)
        def _():
            pl.semaphore_wait(down.at[step - 1], 1)

    barrier = pltpu.get_barrier_semaphore()
    for k in range(1, na):
        pl.semaphore_signal(barrier, inc=1, device_id=a_peer(k), device_id_type=MESH)

    @pl.when(zed + 1 < nz)
    def _():
        pl.semaphore_signal(barrier, inc=1, device_id=z_next(1), device_id_type=MESH)

    @pl.when(zed >= 1)
    def _():
        pl.semaphore_signal(barrier, inc=1, device_id=z_next(-1), device_id_type=MESH)

    greeted = na - 1 + (zed + nz - 1) // nz + (2 * nz - 2 - zed) // nz

    loads = []
    pairs = [(qhid_in, hid.at[pl.ds(ntp, ntok)]), (proj_in, proj), (lens_in, lens)]
    pairs += [(phid.at[p], hid.at[pl.ds(p * plen, plen)]) for p in range(npass)]
    for n, (src, dst) in enumerate(pairs):
        load = pltpu.make_async_copy(src, dst, in_sem.at[n])
        load.start()
        loads.append(load)
    ppad, qpad = sc.shape[1:]
    token = rows_iota((nqi, qpad), 0)
    query = slot_owner(token // ntok) * nquery + lax.rem(token, ntok) // qlen
    pick[...] = jnp.where(query == rows_iota((nqi, qpad), 1), 1.0, 0.0).astype(BF16)
    token_t = rows_iota((qpad, nqi), 1)
    query_t = slot_owner(token_t // ntok) * nquery + lax.rem(token_t, ntok) // qlen
    spread[...] = jnp.where(query_t == rows_iota((qpad, nqi), 0), 1.0, 0.0).astype(BF16)
    tops[...] = jnp.zeros_like(tops)
    sums[...] = jnp.ones_like(sums)
    unit = jnp.where(rows_iota((ntok, LANES), 1) == 0, 1.0, 0.0).astype(BF16)
    loads[0].wait()
    loads[1].wait()
    tok[0] = jnp.dot(hid[ntp : ntp + ntok, :], proj[...], preferred_element_type=F32).astype(BF16)
    pl.semaphore_wait(barrier, greeted)
    tok_copies = share(lambda k: tok.at[0], lambda k: tok.at[k], tok_s, tok_r, blk_peer, nblk)
    half = ntok // 2

    def send_hid(n, k, slot, source, piece):
        start = piece * half
        copy = pltpu.make_async_remote_copy(
            src_ref=hid.at[pl.ds(ntp + source * ntok + start, half)],
            dst_ref=hid.at[pl.ds(ntp + slot * ntok + start, half)],
            send_sem=hid_s.at[n], recv_sem=hid_r.at[n], device_id=blk_peer(k), device_id_type=MESH,
        )
        copy.start()
        return copy

    relayed = paired and nblk == 4
    hid_plan = [(k, k, 0, (k + 1 + turn) % 2) for turn in range(2) for k in range(1, 3 if relayed else nblk)]
    hid_copies = [send_hid(n, *plan) for n, plan in enumerate(hid_plan)]
    if nz > 2:
        tell(1)

    loads[2].wait()
    size = jnp.ones((ppad, LANES), jnp.int32)
    for p in range(npass):
        loads[3 + p].wait()
        vec = jnp.dot(hid[p * plen : (p + 1) * plen, :], proj[...], preferred_element_type=F32).astype(BF16)
        ptok[p, :, :dim] = vec
        out_of = (rows_iota((plen, LANES), 0) >= lens[0, p]) & (rows_iota((plen, LANES), 1) == 0)
        ptok[p, :, dim:] = jnp.where(out_of, FAR, 0.0).astype(BF16)
        ptok_t[p] = vec.T
        size = jnp.where(rows_iota((ppad, LANES), 0) == p, lens[0, p], size)

    def forward(first, count):
        width = count * ntok
        side = jnp.concatenate([tok[k] for k in range(first, first + count)], 0)
        side = jnp.concatenate([side, jnp.concatenate([unit] * count, 0)], 1)
        here = pl.ds(first * ntok, width)
        for p in range(npass):
            a = lax.dot_general(ptok[p], side, NT, preferred_element_type=F32)
            top = jnp.max(a, 0, keepdims=True)
            e = jnp.exp2((a - top) * (LOG2E / temper))
            expo[p, :, here] = e.astype(BF16)
            tops[pl.ds(p, 1), here] = top
            sums[pl.ds(p, 1), here] = jnp.sum(e, 0, keepdims=True)

    forward(0, 1)
    for k in range(1, nblk - 1):
        tok_copies[k - 1].wait_recv()
    if nblk > 2:
        forward(1, nblk - 2)
    if nblk > 1:
        tok_copies[nblk - 2].wait_recv()
        forward(nblk - 1, 1)

    log_size = jnp.log(size.astype(F32))[:, :1]
    pooled = temper * (tops[...] * (1.0 / temper) + jnp.log(sums[...]) - log_size)
    own = split_dot(pooled, pick[...], 3)
    sc[0] = own
    sc_copies = share(lambda k: sc.at[0], lambda k: sc.at[k], sc_s, sc_r, blk_peer, nblk)
    inv = 1.0 / sums[...]
    every_t = jnp.concatenate([tok[k].astype(F32).T for k in range(nblk)], 1)
    for p in range(npass):
        reach[p] = jnp.dot(ptok_t[p], expo[p], preferred_element_type=F32)
    if nz > 2:
        for step in range(1, nz - 1):
            hear(step)
            if step + 1 < nz - 1:
                tell(step + 1)
    relays = []
    if relayed:
        for n, (k, source) in enumerate(((2, 1), (1, 2))):
            hid_copies[n].wait_recv()
            relays.append(send_hid(len(hid_plan) + n, k, 3, source, n))
    for copy in sc_copies:
        copy.wait_recv()

    score = sc[...]
    row = rows_iota(score.shape, 1)
    lane = rows_iota(score.shape, 2)
    slot = rows_iota(score.shape, 0)
    live = row < npass
    hidden_score = jnp.where(live, score, -jnp.inf)
    top = jnp.max(jnp.max(hidden_score, 0), 0, keepdims=True)
    lse = top + jnp.log(jnp.sum(jnp.sum(jnp.exp(hidden_score - top[None]), 0), 0, keepdims=True))
    mine = rows_iota(own.shape, 0) + blk * npass == rows_iota(own.shape, 1)
    dscore = (jnp.exp(sc[0] - lse) - mine.astype(F32)) / total
    factor = split_dot(dscore, spread[...], 3) * inv

    qg_t = reach[0] * factor[0:1]
    for p in range(1, npass):
        qg_t = qg_t + reach[p] * factor[p : p + 1]
    qg_b = qg_t.astype(BF16)
    grads[:, ntp:] = qg_b
    for k in range(1, nblk):
        qsend[k] = qg_b[:, k * ntok : (k + 1) * ntok]
    qg_copies = []

    for p in range(npass):
        side = (every_t * factor[p : p + 1]).astype(BF16)
        g = lax.dot_general(expo[p], side, NT, preferred_element_type=F32)
        pg_v[p] = g
        grads[:, p * plen : (p + 1) * plen] = g.astype(BF16).T

    hit = live & (slot_owner(slot) * npass + row == lane)
    aim = jnp.sum(jnp.sum(jnp.where(hit, score, 0.0), 0), 0, keepdims=True)
    gap = jnp.where(rows_iota(lse.shape, 1) < nq_all, lse - aim, 0.0)
    lo_c[core] = jnp.broadcast_to(jnp.sum(gap, 1, keepdims=True), lo_c.shape[1:])
    lc_copies = share(lambda k: lo_c.at[core], lambda k: lo_c.at[core], lc_s, lc_r, core_peer, ncore)

    for copy in (hid_copies[2:] if relayed else hid_copies) + relays:
        copy.wait_recv()
    hid_copies = hid_copies + relays
    ws_copies = []
    for h in range(parts):
        w = jnp.dot(grads[...], hid[:, h * cols : (h + 1) * cols], preferred_element_type=F32)
        w = w.T.astype(BF16).reshape(na, cols // na, dim)
        wsend[h] = w
        wrecv[h, me_a] = wsend[h, me_a]
        ws_copies.append(share(
            lambda k: wsend.at[h, a_index(k)], lambda k: wrecv.at[h, me_a], ws_s.at[h], ws_r.at[h], a_peer, na
        ))

    qg_copies = share(lambda k: qsend.at[k], lambda k: qrecv.at[k], qg_s, qg_r, blk_peer, nblk)
    for copy in lc_copies:
        copy.wait_recv()
    lo_z[zed] = jnp.sum(lo_c[...], 0)
    lz_copies = share(lambda k: lo_z.at[zed], lambda k: lo_z.at[zed], lz_s, lz_r, z_peer, nz)
    z_copies = []
    for h in range(parts):
        for copy in ws_copies[h]:
            copy.wait_recv()
        zbuf[h, zed] = jnp.sum(wrecv[h].astype(F32), 0).astype(BF16)
        z_copies.append(share(
            lambda k: zbuf.at[h, zed], lambda k: zbuf.at[h, zed], z_s.at[h], z_r.at[h], z_peer, nz
        ))
    for copy in qg_copies:
        copy.wait_recv()
    mine_t = grads[:, ntp : ntp + ntok].astype(F32)
    for k in range(1, nblk):
        mine_t = mine_t + qrecv[k].astype(F32)
    qg_out[...] = mine_t.T
    for copy in lz_copies:
        copy.wait_recv()
    loss_out[...] = jnp.sum(lo_z[...], 0) / total
    c_copies = []
    for h in range(parts):
        for copy in z_copies[h]:
            copy.wait_recv()
        cbuf[h, me_a] = jnp.sum(zbuf[h].astype(F32), 0).astype(BF16)
        c_copies.append(share(
            lambda k: cbuf.at[h, me_a], lambda k: cbuf.at[h, me_a], c_s.at[h], c_r.at[h], a_peer, na
        ))
    for copy in tok_copies + hid_copies + sc_copies + qg_copies + lc_copies + lz_copies:
        copy.wait_send()
    for h in range(parts):
        for copy in ws_copies[h] + z_copies[h]:
            copy.wait_send()
    for h in range(parts):
        for copy in c_copies[h]:
            copy.wait_recv()
        wg_out[h * cols : (h + 1) * cols, :] = cbuf[h].astype(F32).reshape(cols, dim)
    for h in range(parts):
        for copy in c_copies[h]:
            copy.wait_send()


def write_out(qg, pg, wg, loss, qg_out, pg_out, wg_out, loss_out, sem):
    copies = []
    for n, (src, dst) in enumerate(((pg, pg_out), (wg, wg_out), (qg, qg_out))):
        copy = pltpu.make_async_copy(src, dst, sem.at[n])
        copy.start()
        copies.append(copy)
    loss_out[0, 0] = loss[0, 0]
    for copy in copies:
        copy.wait()


def shards(query_hidden, passage_hidden, lengths, projection):
    hidden, dim = projection.shape
    nquery, qlen = query_hidden.shape[1:3]
    npass, plen = passage_hidden.shape[1:3]
    nblk = lax.axis_size("blk")
    nrep = lax.axis_size("rep")
    ncore = 2 if nrep % 2 == 0 else 1
    nz = nrep // ncore
    na = nblk * ncore
    ntok = nquery * qlen
    nqi = nblk * ntok
    ntp = npass * plen
    ppad = -(-npass // 8) * 8
    qpad = -(-nblk * nquery // LANES) * LANES
    parts = 3 if hidden % (3 * 16 * na) == 0 else 1
    deep = hidden // parts // na
    dims = (nblk, nrep, ncore, nquery, qlen, npass, plen)
    vmem = pl.BlockSpec(memory_space=pltpu.VMEM)
    sem = lambda *n: pltpu.SemaphoreType.DMA(tuple(max(i, 1) for i in n))
    flag = pltpu.SemaphoreType.REGULAR((max(nz - 2, 1),))
    pairs = []
    for n in (nblk, nblk, ncore, nz, nblk):
        pairs += [sem(n - 1), sem(n - 1)]
    pairs[2:2] = [sem(2 * nblk), sem(2 * nblk)]
    for n in (na, nz, na):
        pairs += [sem(parts, n - 1), sem(parts, n - 1)]
    held = pl.pallas_call(
        functools.partial(kernel, dims),
        out_shape=(
            pltpu.VMEM((ntok, dim), F32),
            pltpu.VMEM((npass, plen, dim), F32),
            pltpu.VMEM((hidden, dim), F32),
            pltpu.VMEM((8, LANES), F32),
        ),
        in_specs=[
            *[pl.BlockSpec(memory_space=pl.ANY)] * 4,
        ],
        out_specs=(vmem, vmem, vmem, vmem),
        scratch_shapes=[
            pltpu.SMEM((1, npass), jnp.int32),
            pltpu.VMEM((hidden, dim), BF16),
            pltpu.VMEM((nqi, qpad), BF16),
            pltpu.VMEM((qpad, nqi), BF16),
            pltpu.VMEM((nblk, ntok, dim), BF16),
            pltpu.VMEM((npass, plen, dim + LANES), BF16),
            pltpu.VMEM((npass, dim, plen), BF16),
            pltpu.VMEM((ntp + nqi, hidden), BF16),
            pltpu.VMEM((npass, plen, nqi), BF16),
            pltpu.VMEM((npass, dim, nqi), F32),
            pltpu.VMEM((dim, ntp + nqi), BF16),
            pltpu.VMEM((ppad, nqi), F32),
            pltpu.VMEM((ppad, nqi), F32),
            pltpu.VMEM((nblk, ppad, qpad), F32),
            pltpu.VMEM((ncore, 8, LANES), F32),
            pltpu.VMEM((nz, 8, LANES), F32),
            pltpu.VMEM((nblk, dim, ntok), BF16),
            pltpu.VMEM((nblk, dim, ntok), BF16),
            pltpu.VMEM((parts, na, deep, dim), BF16),
            pltpu.VMEM((parts, na, deep, dim), BF16),
            pltpu.VMEM((parts, nz, deep, dim), BF16),
            pltpu.VMEM((parts, na, deep, dim), BF16),
            sem(npass + 3),
            flag,
            flag,
        ] + pairs,
        compiler_params=pltpu.CompilerParams(
            collective_id=0, has_side_effects=True, vmem_limit_bytes=56 << 20
        ),
    )(
        lengths,
        query_hidden.reshape(ntok, hidden),
        projection,
        passage_hidden.reshape(npass, plen, hidden),
    )
    hbm = pl.BlockSpec(memory_space=pl.ANY)
    qg, pg, wg, loss = pl.pallas_call(
        write_out,
        out_shape=(
            jax.ShapeDtypeStruct((ntok, dim), F32),
            jax.ShapeDtypeStruct((npass, plen, dim), F32),
            jax.ShapeDtypeStruct((hidden, dim), F32),
            jax.ShapeDtypeStruct((1, 1), F32),
        ),
        in_specs=[vmem] * 4,
        out_specs=(hbm, hbm, hbm, pl.BlockSpec(memory_space=pltpu.SMEM)),
        scratch_shapes=[sem(3)],
        compiler_params=pltpu.CompilerParams(vmem_limit_bytes=8 << 20),
    )(*[pltpu.with_memory_space_constraint(x, pltpu.VMEM) for x in held])
    return (
        qg.reshape(1, nquery, qlen, dim),
        pg.reshape(1, npass, plen, dim),
        wg,
        loss.reshape(()),
    )


def solution(mesh):
    return jax.shard_map(
        shards,
        mesh=mesh,
        in_specs=(P("rep", "blk", None, None), P("rep", "blk", None, None), P("rep", "blk"), P()),
        out_specs=(P("rep", "blk", None, None), P("rep", "blk", None, None), P(), P()),
        check_vma=False,
    )
```

```python
import functools

import jax
import jax.numpy as jnp
from jax import lax
from jax.experimental import pallas as pl
from jax.experimental.pallas import tpu as pltpu
from jax.sharding import PartitionSpec as P

MESH = pl.DeviceIdType.MESH
F32 = jnp.float32
BF16 = jnp.bfloat16
NT = (((1,), (1,)), ((), ()))

temper = 0.5
LANES = 128
LOG2E = 1.4426950408889634
FAR = -1e30


def rows_iota(shape, dim):
    return lax.broadcasted_iota(jnp.int32, shape, dim)


def split_dot(x, ones, terms):
    out = None
    for _ in range(terms):
        part = x.astype(BF16)
        x = x - part.astype(F32)
        dot = jnp.dot(part, ones, preferred_element_type=F32)
        out = dot if out is None else out + dot
    return out


def kernel(
    dims, lens_in, qhid_in, proj_in, phid, qg_out, pg_v, wg_out, loss_out,
    lens, proj, pick, spread, tok, ptok, ptok_t, hid, expo, reach, grads, tops, sums, sc, lo_c, lo_z, qsend, qrecv,
    wsend, wrecv, zbuf, cbuf,
    in_sem, up, down, tok_s, tok_r, hid_s, hid_r, sc_s, sc_r, lc_s, lc_r, lz_s, lz_r, qg_s, qg_r, ws_s, ws_r,
    z_s, z_r, c_s, c_r,
):
    nblk, nrep, ncore, nquery, qlen, npass, plen = dims
    ntok = nquery * qlen
    nqi = nblk * ntok
    nq_all = nblk * nquery
    ntp = npass * plen
    nz = nrep // ncore
    na = nblk * ncore
    hidden, dim = proj.shape
    total = nq_all * nrep
    parts = wsend.shape[0]
    cols = hidden // parts
    paired = nblk & (nblk - 1) == 0
    blk = lax.axis_index("blk")
    rep = lax.axis_index("rep")
    core = lax.rem(rep, ncore)
    zed = rep // ncore
    me_a = blk * ncore + core

    def blk_at(k):
        if not paired:
            return lax.rem(blk + k, nblk)
        out = 0
        bit = 1
        while bit < nblk:
            out = out + lax.rem(blk // bit + k // bit, 2) * bit
            bit *= 2
        return out

    def slot_owner(slots):
        return slots ^ blk if paired else lax.rem(blk + nblk - slots, nblk)

    def blk_peer(k):
        return (blk_at(k), rep)

    def core_peer(k):
        return (blk, zed * ncore + lax.rem(core + k, ncore))

    def a_index(k):
        return lax.rem(me_a + k, na)

    def a_peer(k):
        other = a_index(k)
        return (other // ncore, zed * ncore + lax.rem(other, ncore))

    def z_peer(k):
        return (blk, lax.rem(zed + k, nz) * ncore + core)

    def z_next(step):
        return (blk, (zed + step) * ncore + core)

    def start_copy(src, dst, send, recv, device):
        copy = pltpu.make_async_remote_copy(
            src_ref=src, dst_ref=dst, send_sem=send, recv_sem=recv, device_id=device, device_id_type=MESH
        )
        copy.start()
        return copy

    def bytes_of(view, send, recv):
        return pltpu.make_async_remote_copy(
            src_ref=view, dst_ref=view, send_sem=send, recv_sem=recv, device_id=a_peer(1), device_id_type=MESH
        )

    def share(src, dst, send, recv, peer, count):
        for k in range(1, count):
            start_copy(src(k), dst(k), send, recv, peer(k))

    def tell(step):
        @pl.when((zed >= step) & (zed + 1 < nz))
        def _():
            pl.semaphore_signal(up.at[step - 1], inc=1, device_id=z_next(1), device_id_type=MESH)

        @pl.when((zed + step < nz) & (zed >= 1))
        def _():
            pl.semaphore_signal(down.at[step - 1], inc=1, device_id=z_next(-1), device_id_type=MESH)

    def hear(step):
        @pl.when(zed >= step + 1)
        def _():
            pl.semaphore_wait(up.at[step - 1], 1)

        @pl.when(zed + step + 1 < nz)
        def _():
            pl.semaphore_wait(down.at[step - 1], 1)

    barrier = pltpu.get_barrier_semaphore()
    for k in range(1, na):
        pl.semaphore_signal(barrier, inc=1, device_id=a_peer(k), device_id_type=MESH)

    @pl.when(zed + 1 < nz)
    def _():
        pl.semaphore_signal(barrier, inc=1, device_id=z_next(1), device_id_type=MESH)

    @pl.when(zed >= 1)
    def _():
        pl.semaphore_signal(barrier, inc=1, device_id=z_next(-1), device_id_type=MESH)

    greeted = na - 1 + (zed + nz - 1) // nz + (2 * nz - 2 - zed) // nz

    loads = []
    pairs = [(qhid_in, hid.at[pl.ds(ntp, ntok)]), (proj_in, proj), (lens_in, lens)]
    pairs += [(phid.at[p], hid.at[pl.ds(p * plen, plen)]) for p in range(npass)]
    for n, (src, dst) in enumerate(pairs):
        load = pltpu.make_async_copy(src, dst, in_sem.at[n])
        load.start()
        loads.append(load)
    ppad, qpad = sc.shape[1:]
    token = rows_iota((nqi, qpad), 0)
    query = slot_owner(token // ntok) * nquery + lax.rem(token, ntok) // qlen
    pick[...] = jnp.where(query == rows_iota((nqi, qpad), 1), 1.0, 0.0).astype(BF16)
    token_t = rows_iota((qpad, nqi), 1)
    query_t = slot_owner(token_t // ntok) * nquery + lax.rem(token_t, ntok) // qlen
    spread[...] = jnp.where(query_t == rows_iota((qpad, nqi), 0), 1.0, 0.0).astype(BF16)
    tops[...] = jnp.zeros_like(tops)
    sums[...] = jnp.ones_like(sums)
    unit = jnp.where(rows_iota((ntok, LANES), 1) == 0, 1.0, 0.0).astype(BF16)
    loads[0].wait()
    loads[1].wait()
    tok[0] = jnp.dot(hid[ntp : ntp + ntok, :], proj[...], preferred_element_type=F32).astype(BF16)
    pl.semaphore_wait(barrier, greeted)
    tok_copies = [start_copy(tok.at[0], tok.at[k], tok_s.at[k - 1], tok_r.at[k - 1], blk_peer(k)) for k in range(1, nblk)]
    half = ntok // 2

    def send_hid(k, slot, source, piece, recv):
        start = piece * half
        start_copy(
            hid.at[pl.ds(ntp + source * ntok + start, half)], hid.at[pl.ds(ntp + slot * ntok + start, half)],
            hid_s.at[0], recv, blk_peer(k),
        )

    relayed = paired and nblk == 4
    near = 3 if relayed else nblk
    for turn in range(2):
        for k in range(1, near):
            send_hid(k, k, 0, (k + 1 + turn) % 2, hid_r.at[turn])
    if nz > 2:
        tell(1)

    loads[2].wait()
    size = jnp.ones((ppad, LANES), jnp.int32)
    for p in range(npass):
        loads[3 + p].wait()
        vec = jnp.dot(hid[p * plen : (p + 1) * plen, :], proj[...], preferred_element_type=F32).astype(BF16)
        ptok[p, :, :dim] = vec
        out_of = (rows_iota((plen, LANES), 0) >= lens[0, p]) & (rows_iota((plen, LANES), 1) == 0)
        ptok[p, :, dim:] = jnp.where(out_of, FAR, 0.0).astype(BF16)
        ptok_t[p] = vec.T
        size = jnp.where(rows_iota((ppad, LANES), 0) == p, lens[0, p], size)

    def forward(first, count):
        width = count * ntok
        side = jnp.concatenate([tok[k] for k in range(first, first + count)], 0)
        side = jnp.concatenate([side, jnp.concatenate([unit] * count, 0)], 1)
        here = pl.ds(first * ntok, width)
        for p in range(npass):
            a = lax.dot_general(ptok[p], side, NT, preferred_element_type=F32)
            top = jnp.max(a, 0, keepdims=True)
            e = jnp.exp2((a - top) * (LOG2E / temper))
            expo[p, :, here] = e.astype(BF16)
            tops[pl.ds(p, 1), here] = top
            sums[pl.ds(p, 1), here] = jnp.sum(e, 0, keepdims=True)

    forward(0, 1)
    for k in range(1, nblk - 1):
        tok_copies[k - 1].wait_recv()
    if nblk > 2:
        forward(1, nblk - 2)
    if nblk > 1:
        tok_copies[nblk - 2].wait_recv()
        forward(nblk - 1, 1)

    log_size = jnp.log(size.astype(F32))[:, :1]
    pooled = temper * (tops[...] * (1.0 / temper) + jnp.log(sums[...]) - log_size)
    own = split_dot(pooled, pick[...], 3)
    sc[0] = own
    share(lambda k: sc.at[0], lambda k: sc.at[k], sc_s.at[0], sc_r.at[0], blk_peer, nblk)
    sc_all = bytes_of(sc.at[pl.ds(0, nblk - 1)], sc_s.at[0], sc_r.at[0])
    inv = 1.0 / sums[...]
    every_t = jnp.concatenate([tok[k].astype(F32).T for k in range(nblk)], 1)
    if nblk > 1:
        bytes_of(hid.at[pl.ds(ntp, (near - 1) * half)], hid_s.at[0], hid_r.at[0]).wait_recv()
    if relayed:
        send_hid(2, 3, 1, 0, hid_r.at[1])
        send_hid(1, 3, 2, 1, hid_r.at[1])
    for p in range(npass):
        reach[p] = jnp.dot(ptok_t[p], expo[p], preferred_element_type=F32)
    if nz > 2:
        for step in range(1, nz - 1):
            hear(step)
            if step + 1 < nz - 1:
                tell(step + 1)
    if nblk > 1:
        sc_all.wait_recv()

    score = sc[...]
    row = rows_iota(score.shape, 1)
    lane = rows_iota(score.shape, 2)
    slot = rows_iota(score.shape, 0)
    live = row < npass
    hidden_score = jnp.where(live, score, -jnp.inf)
    top = jnp.max(jnp.max(hidden_score, 0), 0, keepdims=True)
    lse = top + jnp.log(jnp.sum(jnp.sum(jnp.exp(hidden_score - top[None]), 0), 0, keepdims=True))
    mine = rows_iota(own.shape, 0) + blk * npass == rows_iota(own.shape, 1)
    dscore = (jnp.exp(sc[0] - lse) - mine.astype(F32)) / total
    factor = split_dot(dscore, spread[...], 3) * inv

    qg_t = reach[0] * factor[0:1]
    for p in range(1, npass):
        qg_t = qg_t + reach[p] * factor[p : p + 1]
    qg_b = qg_t.astype(BF16)
    grads[:, ntp:] = qg_b
    for k in range(1, nblk):
        qsend[k] = qg_b[:, k * ntok : (k + 1) * ntok]

    for p in range(npass):
        side = (every_t * factor[p : p + 1]).astype(BF16)
        g = lax.dot_general(expo[p], side, NT, preferred_element_type=F32)
        pg_v[p] = g
        grads[:, p * plen : (p + 1) * plen] = g.astype(BF16).T

    hit = live & (slot_owner(slot) * npass + row == lane)
    aim = jnp.sum(jnp.sum(jnp.where(hit, score, 0.0), 0), 0, keepdims=True)
    gap = jnp.where(rows_iota(lse.shape, 1) < nq_all, lse - aim, 0.0)
    lo_c[core] = jnp.broadcast_to(jnp.sum(gap, 1, keepdims=True), lo_c.shape[1:])
    share(lambda k: lo_c.at[core], lambda k: lo_c.at[core], lc_s.at[0], lc_r.at[0], core_peer, ncore)
    lc_all = bytes_of(lo_c.at[pl.ds(0, ncore - 1)], lc_s.at[0], lc_r.at[0])

    late = near - 1 + 2 * relayed
    if nblk > 1:
        bytes_of(hid.at[pl.ds(ntp, late * half)], hid_s.at[0], hid_r.at[1]).wait_recv()
    for h in range(parts):
        w = jnp.dot(grads[...], hid[:, h * cols : (h + 1) * cols], preferred_element_type=F32)
        w = w.T.astype(BF16).reshape(na, cols // na, dim)
        wsend[h] = w
        wrecv[h, me_a] = wsend[h, me_a]
        share(lambda k: wsend.at[h, a_index(k)], lambda k: wrecv.at[h, me_a], ws_s.at[0], ws_r.at[h], a_peer, na)

    share(lambda k: qsend.at[k], lambda k: qrecv.at[k], qg_s.at[0], qg_r.at[0], blk_peer, nblk)
    qg_all = bytes_of(qrecv.at[pl.ds(0, nblk - 1)], qg_s.at[0], qg_r.at[0])
    if ncore > 1:
        lc_all.wait_recv()
    lo_z[zed] = jnp.sum(lo_c[...], 0)
    share(lambda k: lo_z.at[zed], lambda k: lo_z.at[zed], lz_s.at[0], lz_r.at[0], z_peer, nz)
    lz_all = bytes_of(lo_z.at[pl.ds(0, nz - 1)], lz_s.at[0], lz_r.at[0])
    for h in range(parts):
        if na > 1:
            bytes_of(wrecv.at[h, pl.ds(0, na - 1)], ws_s.at[0], ws_r.at[h]).wait_recv()
        zbuf[h, zed] = jnp.sum(wrecv[h].astype(F32), 0).astype(BF16)
        share(lambda k: zbuf.at[h, zed], lambda k: zbuf.at[h, zed], z_s.at[0], z_r.at[h], z_peer, nz)
    if nblk > 1:
        qg_all.wait_recv()
    mine_t = grads[:, ntp : ntp + ntok].astype(F32)
    for k in range(1, nblk):
        mine_t = mine_t + qrecv[k].astype(F32)
    qg_out[...] = mine_t.T
    if nz > 1:
        lz_all.wait_recv()
    loss_out[...] = jnp.sum(lo_z[...], 0) / total
    for h in range(parts):
        if nz > 1:
            bytes_of(zbuf.at[h, pl.ds(0, nz - 1)], z_s.at[0], z_r.at[h]).wait_recv()
        cbuf[h, me_a] = jnp.sum(zbuf[h].astype(F32), 0).astype(BF16)
        share(lambda k: cbuf.at[h, me_a], lambda k: cbuf.at[h, me_a], c_s.at[0], c_r.at[h], a_peer, na)
    for copy in tok_copies:
        copy.wait_send()
    if nblk > 1:
        bytes_of(hid.at[pl.ds(ntp, (2 * (near - 1) + 2 * relayed) * half)], hid_s.at[0], hid_r.at[0]).wait_send()
        sc_all.wait_send()
        qg_all.wait_send()
    if ncore > 1:
        lc_all.wait_send()
    if na > 1:
        bytes_of(wsend.at[:, pl.ds(0, na - 1)], ws_s.at[0], ws_r.at[0]).wait_send()
    if nz > 1:
        lz_all.wait_send()
        bytes_of(zbuf.at[:, pl.ds(0, nz - 1)], z_s.at[0], z_r.at[0]).wait_send()
    for h in range(parts):
        if na > 1:
            bytes_of(cbuf.at[h, pl.ds(0, na - 1)], c_s.at[0], c_r.at[h]).wait_recv()
        wg_out[h * cols : (h + 1) * cols, :] = cbuf[h].astype(F32).reshape(cols, dim)
    if na > 1:
        bytes_of(cbuf.at[:, pl.ds(0, na - 1)], c_s.at[0], c_r.at[0]).wait_send()


def write_out(qg, pg, wg, loss, qg_out, pg_out, wg_out, loss_out, sem):
    copies = []
    for n, (src, dst) in enumerate(((pg, pg_out), (wg, wg_out), (qg, qg_out))):
        copy = pltpu.make_async_copy(src, dst, sem.at[n])
        copy.start()
        copies.append(copy)
    loss_out[0, 0] = loss[0, 0]
    for copy in copies:
        copy.wait()


def shards(query_hidden, passage_hidden, lengths, projection):
    hidden, dim = projection.shape
    nquery, qlen = query_hidden.shape[1:3]
    npass, plen = passage_hidden.shape[1:3]
    nblk = lax.axis_size("blk")
    nrep = lax.axis_size("rep")
    ncore = 2 if nrep % 2 == 0 else 1
    nz = nrep // ncore
    na = nblk * ncore
    ntok = nquery * qlen
    nqi = nblk * ntok
    ntp = npass * plen
    ppad = -(-npass // 8) * 8
    qpad = -(-nblk * nquery // LANES) * LANES
    parts = 3 if hidden % (3 * 16 * na) == 0 else 1
    deep = hidden // parts // na
    dims = (nblk, nrep, ncore, nquery, qlen, npass, plen)
    vmem = pl.BlockSpec(memory_space=pltpu.VMEM)
    sem = lambda *n: pltpu.SemaphoreType.DMA(tuple(max(i, 1) for i in n))
    flag = pltpu.SemaphoreType.REGULAR((max(nz - 2, 1),))
    pairs = [sem(nblk - 1), sem(nblk - 1), sem(1), sem(2)]
    pairs += [sem(1)] * 8
    pairs += [sem(1), sem(parts)] * 3
    held = pl.pallas_call(
        functools.partial(kernel, dims),
        out_shape=(
            pltpu.VMEM((ntok, dim), F32),
            pltpu.VMEM((npass, plen, dim), F32),
            pltpu.VMEM((hidden, dim), F32),
            pltpu.VMEM((8, LANES), F32),
        ),
        in_specs=[
            *[pl.BlockSpec(memory_space=pl.ANY)] * 4,
        ],
        out_specs=(vmem, vmem, vmem, vmem),
        scratch_shapes=[
            pltpu.SMEM((1, npass), jnp.int32),
            pltpu.VMEM((hidden, dim), BF16),
            pltpu.VMEM((nqi, qpad), BF16),
            pltpu.VMEM((qpad, nqi), BF16),
            pltpu.VMEM((nblk, ntok, dim), BF16),
            pltpu.VMEM((npass, plen, dim + LANES), BF16),
            pltpu.VMEM((npass, dim, plen), BF16),
            pltpu.VMEM((ntp + nqi, hidden), BF16),
            pltpu.VMEM((npass, plen, nqi), BF16),
            pltpu.VMEM((npass, dim, nqi), F32),
            pltpu.VMEM((dim, ntp + nqi), BF16),
            pltpu.VMEM((ppad, nqi), F32),
            pltpu.VMEM((ppad, nqi), F32),
            pltpu.VMEM((nblk, ppad, qpad), F32),
            pltpu.VMEM((ncore, 8, LANES), F32),
            pltpu.VMEM((nz, 8, LANES), F32),
            pltpu.VMEM((nblk, dim, ntok), BF16),
            pltpu.VMEM((nblk, dim, ntok), BF16),
            pltpu.VMEM((parts, na, deep, dim), BF16),
            pltpu.VMEM((parts, na, deep, dim), BF16),
            pltpu.VMEM((parts, nz, deep, dim), BF16),
            pltpu.VMEM((parts, na, deep, dim), BF16),
            sem(npass + 3),
            flag,
            flag,
        ] + pairs,
        compiler_params=pltpu.CompilerParams(
            collective_id=0, has_side_effects=True, vmem_limit_bytes=56 << 20
        ),
    )(
        lengths,
        query_hidden.reshape(ntok, hidden),
        projection,
        passage_hidden.reshape(npass, plen, hidden),
    )
    hbm = pl.BlockSpec(memory_space=pl.ANY)
    qg, pg, wg, loss = pl.pallas_call(
        write_out,
        out_shape=(
            jax.ShapeDtypeStruct((ntok, dim), F32),
            jax.ShapeDtypeStruct((npass, plen, dim), F32),
            jax.ShapeDtypeStruct((hidden, dim), F32),
            jax.ShapeDtypeStruct((1, 1), F32),
        ),
        in_specs=[vmem] * 4,
        out_specs=(hbm, hbm, hbm, pl.BlockSpec(memory_space=pltpu.SMEM)),
        scratch_shapes=[sem(3)],
        compiler_params=pltpu.CompilerParams(vmem_limit_bytes=8 << 20),
    )(*[pltpu.with_memory_space_constraint(x, pltpu.VMEM) for x in held])
    return (
        qg.reshape(1, nquery, qlen, dim),
        pg.reshape(1, npass, plen, dim),
        wg,
        loss.reshape(()),
    )


def solution(mesh):
    return jax.shard_map(
        shards,
        mesh=mesh,
        in_specs=(P("rep", "blk", None, None), P("rep", "blk", None, None), P("rep", "blk"), P()),
        out_specs=(P("rep", "blk", None, None), P("rep", "blk", None, None), P(), P()),
        check_vma=False,
    )
```

```python
import functools

import jax
import jax.numpy as jnp
from jax import lax
from jax.experimental import pallas as pl
from jax.experimental.pallas import tpu as pltpu
from jax.sharding import PartitionSpec as P

MESH = pl.DeviceIdType.MESH
F32 = jnp.float32
BF16 = jnp.bfloat16
NT = (((1,), (1,)), ((), ()))
TN = (((0,), (0,)), ((), ()))

temper = 0.5
LANES = 128
LOG2E = 1.4426950408889634
FAR = -1e30


def rows_iota(shape, dim):
    return lax.broadcasted_iota(jnp.int32, shape, dim)


def split_dot(x, ones, terms):
    out = None
    for _ in range(terms):
        part = x.astype(BF16)
        x = x - part.astype(F32)
        dot = jnp.dot(part, ones, preferred_element_type=F32)
        out = dot if out is None else out + dot
    return out


def kernel(
    dims, lens_in, qhid_in, proj_in, phid, qg_out, pg_v, wg_out, loss_out,
    lens, proj, pick, spread, tok, ptok, ptok_t, hid, expo, reach, grads, drawn, tops, sums, sc, lo_c, lo_z, qsend, qrecv,
    wsend, wrecv, zbuf, cbuf,
    in_sem, up, down, tok_s, tok_r, hid_s, hid_r, sc_s, sc_r, lc_s, lc_r, lz_s, lz_r, qg_s, qg_r, ws_s, ws_r,
    z_s, z_r, c_s, c_r,
):
    nblk, nrep, ncore, nquery, qlen, npass, plen = dims
    ntok = nquery * qlen
    nqi = nblk * ntok
    nq_all = nblk * nquery
    ntp = npass * plen
    nfac = npass * nqi
    nz = nrep // ncore
    na = nblk * ncore
    hidden, dim = proj.shape
    total = nq_all * nrep
    parts = wsend.shape[0]
    cols = hidden // parts
    paired = nblk & (nblk - 1) == 0
    blk = lax.axis_index("blk")
    rep = lax.axis_index("rep")
    core = lax.rem(rep, ncore)
    zed = rep // ncore
    me_a = blk * ncore + core

    def mixed(index, k, count):
        if count & (count - 1):
            return lax.rem(index + k, count)
        out = 0
        bit = 1
        while bit < count:
            out = out + lax.rem(index // bit + k // bit, 2) * bit
            bit *= 2
        return out

    def slot_owner(slots):
        return slots ^ blk if paired else lax.rem(blk + nblk - slots, nblk)

    def blk_peer(k):
        return (mixed(blk, k, nblk), rep)

    def core_peer(k):
        return (blk, zed * ncore + lax.rem(core + k, ncore))

    def a_index(k):
        return mixed(me_a, k, na)

    def a_peer(k):
        other = a_index(k)
        return (other // ncore, zed * ncore + lax.rem(other, ncore))

    def z_peer(k):
        return (blk, mixed(zed, k, nz) * ncore + core)

    def z_next(step):
        return (blk, (zed + step) * ncore + core)

    def start_copy(src, dst, send, recv, device):
        copy = pltpu.make_async_remote_copy(
            src_ref=src, dst_ref=dst, send_sem=send, recv_sem=recv, device_id=device, device_id_type=MESH
        )
        copy.start()
        return copy

    def bytes_of(view, send, recv):
        return pltpu.make_async_remote_copy(
            src_ref=view, dst_ref=view, send_sem=send, recv_sem=recv, device_id=a_peer(1), device_id_type=MESH
        )

    def share(src, dst, send, recv, peer, count):
        for k in range(count - 1, 0, -1):
            start_copy(src(k), dst(k), send, recv, peer(k))

    def tell(step):
        @pl.when((zed >= step) & (zed + 1 < nz))
        def _():
            pl.semaphore_signal(up.at[step - 1], inc=1, device_id=z_next(1), device_id_type=MESH)

        @pl.when((zed + step < nz) & (zed >= 1))
        def _():
            pl.semaphore_signal(down.at[step - 1], inc=1, device_id=z_next(-1), device_id_type=MESH)

    def hear(step):
        @pl.when(zed >= step + 1)
        def _():
            pl.semaphore_wait(up.at[step - 1], 1)

        @pl.when(zed + step + 1 < nz)
        def _():
            pl.semaphore_wait(down.at[step - 1], 1)

    barrier = pltpu.get_barrier_semaphore()
    for k in range(na - 1, 0, -1):
        pl.semaphore_signal(barrier, inc=1, device_id=a_peer(k), device_id_type=MESH)

    @pl.when(zed + 1 < nz)
    def _():
        pl.semaphore_signal(barrier, inc=1, device_id=z_next(1), device_id_type=MESH)

    @pl.when(zed >= 1)
    def _():
        pl.semaphore_signal(barrier, inc=1, device_id=z_next(-1), device_id_type=MESH)

    greeted = na - 1 + (zed + nz - 1) // nz + (2 * nz - 2 - zed) // nz

    loads = []
    pairs = [(qhid_in, hid.at[pl.ds(ntp, ntok)]), (proj_in, proj), (lens_in, lens)]
    pairs += [(phid.at[p], hid.at[pl.ds(p * plen, plen)]) for p in range(npass)]
    for n, (src, dst) in enumerate(pairs):
        load = pltpu.make_async_copy(src, dst, in_sem.at[n])
        load.start()
        loads.append(load)
    ppad, qpad = sc.shape[1:]
    token = rows_iota((nqi, qpad), 0)
    query = slot_owner(token // ntok) * nquery + lax.rem(token, ntok) // qlen
    pick[...] = jnp.where(query == rows_iota((nqi, qpad), 1), 1.0, 0.0).astype(BF16)
    token_t = rows_iota((qpad, nqi), 1)
    query_t = slot_owner(token_t // ntok) * nquery + lax.rem(token_t, ntok) // qlen
    spread[...] = jnp.where(query_t == rows_iota((qpad, nqi), 0), 1.0, 0.0).astype(BF16)
    tops[...] = jnp.zeros_like(tops)
    sums[...] = jnp.ones_like(sums)
    unit = jnp.where(rows_iota((ntok, LANES), 1) == 0, 1.0, 0.0).astype(BF16)
    loads[0].wait()
    loads[1].wait()
    tok[0] = jnp.dot(hid[ntp : ntp + ntok, :], proj[...], preferred_element_type=F32).astype(BF16)
    pl.semaphore_wait(barrier, greeted)
    tok_copies = [start_copy(tok.at[0], tok.at[k], tok_s.at[k - 1], tok_r.at[k - 1], blk_peer(k)) for k in range(nblk - 1, 0, -1)][::-1]
    relayed = paired and nblk == 4
    half = ntok // 2

    def send_hid(h, k, slot, source, start, count, recv):
        here = pl.ds(h * cols, cols)
        start_copy(
            hid.at[pl.ds(ntp + source * ntok + start, count), here],
            hid.at[pl.ds(ntp + slot * ntok + start, count), here],
            hid_s.at[0], hid_r.at[recv], blk_peer(k),
        )

    def hid_bytes(h, rows, recv):
        return bytes_of(hid.at[pl.ds(ntp, rows), pl.ds(h * cols, cols)], hid_s.at[0], hid_r.at[recv])

    def relay(h):
        if relayed:
            hid_bytes(h, 2 * half, h).wait_recv()
            send_hid(h, 2, 3, 1, 0, half, parts + h)
            send_hid(h, 1, 3, 2, half, half, parts + h)

    if relayed:
        for turn in range(2):
            for h in range(parts):
                for k in (1, 2):
                    send_hid(h, k, k, 0, (k + 1 + turn) % 2 * half, half, turn * parts + h)
        late_rows, sent_rows = 4 * half, 6 * half
    else:
        for h in range(parts):
            for k in range(1, nblk):
                send_hid(h, k, k, 0, 0, ntok, parts + h)
        late_rows = sent_rows = (nblk - 1) * ntok
    if nz > 2:
        tell(1)

    loads[2].wait()
    size = jnp.ones((ppad, LANES), jnp.int32)
    for p in range(npass):
        loads[3 + p].wait()
        vec = jnp.dot(hid[p * plen : (p + 1) * plen, :], proj[...], preferred_element_type=F32).astype(BF16)
        ptok[p, :, :dim] = vec
        out_of = (rows_iota((plen, LANES), 0) >= lens[0, p]) & (rows_iota((plen, LANES), 1) == 0)
        ptok[p, :, dim:] = jnp.where(out_of, FAR, 0.0).astype(BF16)
        ptok_t[p] = vec.T
        size = jnp.where(rows_iota((ppad, LANES), 0) == p, lens[0, p], size)

    def forward(first, count):
        width = count * ntok
        side = jnp.concatenate([tok[k] for k in range(first, first + count)], 0)
        side = jnp.concatenate([side, jnp.concatenate([unit] * count, 0)], 1)
        here = pl.ds(first * ntok, width)
        for p in range(npass):
            a = lax.dot_general(ptok[p], side, NT, preferred_element_type=F32)
            top = jnp.max(a, 0, keepdims=True)
            e = jnp.exp2((a - top) * (LOG2E / temper))
            expo[p, :, here] = e.astype(BF16)
            tops[pl.ds(p, 1), here] = top
            sums[pl.ds(p, 1), here] = jnp.sum(e, 0, keepdims=True)

    def collect(first, count):
        width = count * ntok
        for p in range(npass):
            m = lax.dot_general(
                expo[p, :, pl.ds(first * ntok, width)], hid[p * plen : (p + 1) * plen, :], TN,
                preferred_element_type=F32,
            )
            drawn[pl.ds(p * nqi + first * ntok, width), :] = m.astype(BF16)

    forward(0, 1)
    collect(0, 1)
    for k in range(1, nblk - 1):
        tok_copies[k - 1].wait_recv()
    if nblk > 2:
        forward(1, nblk - 2)
    if nblk > 1:
        tok_copies[nblk - 2].wait_recv()
        forward(nblk - 1, 1)

    log_size = jnp.log(size.astype(F32))[:, :1]
    pooled = temper * (tops[...] * (1.0 / temper) + jnp.log(sums[...]) - log_size)
    own = split_dot(pooled, pick[...], 3)
    sc[0] = own
    share(lambda k: sc.at[0], lambda k: sc.at[k], sc_s.at[0], sc_r.at[0], blk_peer, nblk)
    sc_all = bytes_of(sc.at[pl.ds(0, nblk - 1)], sc_s.at[0], sc_r.at[0])
    inv = 1.0 / sums[...]
    every_t = jnp.concatenate([tok[k].astype(F32).T for k in range(nblk)], 1)
    relay(0)
    later = list(range(1, parts))
    for p in range(npass):
        reach[p] = jnp.dot(ptok_t[p], expo[p], preferred_element_type=F32)
        if later and p % 2 == 0:
            relay(later.pop(0))
    for h in later:
        relay(h)
    if nblk > 1:
        collect(1, nblk - 1)
    if nz > 2:
        for step in range(1, nz - 1):
            hear(step)
            if step + 1 < nz - 1:
                tell(step + 1)
    if nblk > 1:
        sc_all.wait_recv()

    score = sc[...]
    row = rows_iota(score.shape, 1)
    lane = rows_iota(score.shape, 2)
    slot = rows_iota(score.shape, 0)
    live = row < npass
    hidden_score = jnp.where(live, score, -jnp.inf)
    top = jnp.max(jnp.max(hidden_score, 0), 0, keepdims=True)
    lse = top + jnp.log(jnp.sum(jnp.sum(jnp.exp(hidden_score - top[None]), 0), 0, keepdims=True))
    mine = rows_iota(own.shape, 0) + blk * npass == rows_iota(own.shape, 1)
    dscore = (jnp.exp(sc[0] - lse) - mine.astype(F32)) / total
    factor = split_dot(dscore, spread[...], 3) * inv

    for p in range(npass):
        grads[:, p * nqi : (p + 1) * nqi] = (every_t * factor[p : p + 1]).astype(BF16)
    qg_t = reach[0] * factor[0:1]
    for p in range(1, npass):
        qg_t = qg_t + reach[p] * factor[p : p + 1]
    qg_b = qg_t.astype(BF16)
    grads[:, nfac:] = qg_b
    for k in range(1, nblk):
        qsend[k] = qg_b[:, k * ntok : (k + 1) * ntok]

    for h in range(parts):
        here = slice(h * cols, (h + 1) * cols)
        w = jnp.dot(grads[:, :nfac], drawn[:, here], preferred_element_type=F32)
        if nblk > 1:
            hid_bytes(h, late_rows, parts + h).wait_recv()
        w = w + jnp.dot(grads[:, nfac:], hid[ntp:, here], preferred_element_type=F32)
        w = w.T.astype(BF16).reshape(na, cols // na, dim)
        wsend[h] = w
        wrecv[h, me_a] = wsend[h, me_a]
        share(lambda k: wsend.at[h, a_index(k)], lambda k: wrecv.at[h, me_a], ws_s.at[0], ws_r.at[h], a_peer, na)

    share(lambda k: qsend.at[k], lambda k: qrecv.at[k], qg_s.at[0], qg_r.at[0], blk_peer, nblk)
    qg_all = bytes_of(qrecv.at[pl.ds(0, nblk - 1)], qg_s.at[0], qg_r.at[0])

    hit = live & (slot_owner(slot) * npass + row == lane)
    aim = jnp.sum(jnp.sum(jnp.where(hit, score, 0.0), 0), 0, keepdims=True)
    gap = jnp.where(rows_iota(lse.shape, 1) < nq_all, lse - aim, 0.0)
    lo_c[core] = jnp.broadcast_to(jnp.sum(gap, 1, keepdims=True), lo_c.shape[1:])
    share(lambda k: lo_c.at[core], lambda k: lo_c.at[core], lc_s.at[0], lc_r.at[0], core_peer, ncore)
    lc_all = bytes_of(lo_c.at[pl.ds(0, ncore - 1)], lc_s.at[0], lc_r.at[0])
    for p in range(npass):
        pg_v[p] = lax.dot_general(
            expo[p], grads[:, p * nqi : (p + 1) * nqi], NT, preferred_element_type=F32
        )
    if ncore > 1:
        lc_all.wait_recv()
    lo_z[zed] = jnp.sum(lo_c[...], 0)
    share(lambda k: lo_z.at[zed], lambda k: lo_z.at[zed], lz_s.at[0], lz_r.at[0], z_peer, nz)
    lz_all = bytes_of(lo_z.at[pl.ds(0, nz - 1)], lz_s.at[0], lz_r.at[0])
    for h in range(parts):
        if na > 1:
            bytes_of(wrecv.at[h, pl.ds(0, na - 1)], ws_s.at[0], ws_r.at[h]).wait_recv()
        zbuf[h, zed] = jnp.sum(wrecv[h].astype(F32), 0).astype(BF16)
        share(lambda k: zbuf.at[h, zed], lambda k: zbuf.at[h, zed], z_s.at[0], z_r.at[h], z_peer, nz)
    if nblk > 1:
        qg_all.wait_recv()
    mine_t = grads[:, nfac : nfac + ntok].astype(F32)
    for k in range(1, nblk):
        mine_t = mine_t + qrecv[k].astype(F32)
    qg_out[...] = mine_t.T
    if nz > 1:
        lz_all.wait_recv()
    loss_out[...] = jnp.sum(lo_z[...], 0) / total
    for h in range(parts):
        if nz > 1:
            bytes_of(zbuf.at[h, pl.ds(0, nz - 1)], z_s.at[0], z_r.at[h]).wait_recv()
        cbuf[h, me_a] = jnp.sum(zbuf[h].astype(F32), 0).astype(BF16)
        share(lambda k: cbuf.at[h, me_a], lambda k: cbuf.at[h, me_a], c_s.at[0], c_r.at[h], a_peer, na)
    for copy in tok_copies:
        copy.wait_send()
    if nblk > 1:
        bytes_of(hid.at[pl.ds(ntp, sent_rows)], hid_s.at[0], hid_r.at[0]).wait_send()
        sc_all.wait_send()
        qg_all.wait_send()
    if ncore > 1:
        lc_all.wait_send()
    if na > 1:
        bytes_of(wsend.at[:, pl.ds(0, na - 1)], ws_s.at[0], ws_r.at[0]).wait_send()
    if nz > 1:
        lz_all.wait_send()
        bytes_of(zbuf.at[:, pl.ds(0, nz - 1)], z_s.at[0], z_r.at[0]).wait_send()
    for h in range(parts):
        if na > 1:
            bytes_of(cbuf.at[h, pl.ds(0, na - 1)], c_s.at[0], c_r.at[h]).wait_recv()
        wg_out[h * cols : (h + 1) * cols, :] = cbuf[h].astype(F32).reshape(cols, dim)
    if na > 1:
        bytes_of(cbuf.at[:, pl.ds(0, na - 1)], c_s.at[0], c_r.at[0]).wait_send()


def write_out(qg, pg, wg, loss, qg_out, pg_out, wg_out, loss_out, sem):
    copies = []
    for n, (src, dst) in enumerate(((pg, pg_out), (wg, wg_out), (qg, qg_out))):
        copy = pltpu.make_async_copy(src, dst, sem.at[n])
        copy.start()
        copies.append(copy)
    loss_out[0, 0] = loss[0, 0]
    for copy in copies:
        copy.wait()


def shards(query_hidden, passage_hidden, lengths, projection):
    hidden, dim = projection.shape
    nquery, qlen = query_hidden.shape[1:3]
    npass, plen = passage_hidden.shape[1:3]
    nblk = lax.axis_size("blk")
    nrep = lax.axis_size("rep")
    ncore = 2 if nrep % 2 == 0 else 1
    nz = nrep // ncore
    na = nblk * ncore
    ntok = nquery * qlen
    nqi = nblk * ntok
    ntp = npass * plen
    ppad = -(-npass // 8) * 8
    qpad = -(-nblk * nquery // LANES) * LANES
    parts = 3 if hidden % (3 * 16 * na) == 0 else 1
    deep = hidden // parts // na
    dims = (nblk, nrep, ncore, nquery, qlen, npass, plen)
    vmem = pl.BlockSpec(memory_space=pltpu.VMEM)
    sem = lambda *n: pltpu.SemaphoreType.DMA(tuple(max(i, 1) for i in n))
    flag = pltpu.SemaphoreType.REGULAR((max(nz - 2, 1),))
    pairs = [sem(nblk - 1), sem(nblk - 1), sem(1), sem(2 * parts)]
    pairs += [sem(1)] * 8
    pairs += [sem(1), sem(parts)] * 3
    held = pl.pallas_call(
        functools.partial(kernel, dims),
        out_shape=(
            pltpu.VMEM((ntok, dim), F32),
            pltpu.VMEM((npass, plen, dim), F32),
            pltpu.VMEM((hidden, dim), F32),
            pltpu.VMEM((8, LANES), F32),
        ),
        in_specs=[
            *[pl.BlockSpec(memory_space=pl.ANY)] * 4,
        ],
        out_specs=(vmem, vmem, vmem, vmem),
        scratch_shapes=[
            pltpu.SMEM((1, npass), jnp.int32),
            pltpu.VMEM((hidden, dim), BF16),
            pltpu.VMEM((nqi, qpad), BF16),
            pltpu.VMEM((qpad, nqi), BF16),
            pltpu.VMEM((nblk, ntok, dim), BF16),
            pltpu.VMEM((npass, plen, dim + LANES), BF16),
            pltpu.VMEM((npass, dim, plen), BF16),
            pltpu.VMEM((ntp + nqi, hidden), BF16),
            pltpu.VMEM((npass, plen, nqi), BF16),
            pltpu.VMEM((npass, dim, nqi), F32),
            pltpu.VMEM((dim, npass * nqi + nqi), BF16),
            pltpu.VMEM((npass * nqi, hidden), BF16),
            pltpu.VMEM((ppad, nqi), F32),
            pltpu.VMEM((ppad, nqi), F32),
            pltpu.VMEM((nblk, ppad, qpad), F32),
            pltpu.VMEM((ncore, 8, LANES), F32),
            pltpu.VMEM((nz, 8, LANES), F32),
            pltpu.VMEM((nblk, dim, ntok), BF16),
            pltpu.VMEM((nblk, dim, ntok), BF16),
            pltpu.VMEM((parts, na, deep, dim), BF16),
            pltpu.VMEM((parts, na, deep, dim), BF16),
            pltpu.VMEM((parts, nz, deep, dim), BF16),
            pltpu.VMEM((parts, na, deep, dim), BF16),
            sem(npass + 3),
            flag,
            flag,
        ] + pairs,
        compiler_params=pltpu.CompilerParams(
            collective_id=0, has_side_effects=True, vmem_limit_bytes=56 << 20
        ),
    )(
        lengths,
        query_hidden.reshape(ntok, hidden),
        projection,
        passage_hidden.reshape(npass, plen, hidden),
    )
    hbm = pl.BlockSpec(memory_space=pl.ANY)
    qg, pg, wg, loss = pl.pallas_call(
        write_out,
        out_shape=(
            jax.ShapeDtypeStruct((ntok, dim), F32),
            jax.ShapeDtypeStruct((npass, plen, dim), F32),
            jax.ShapeDtypeStruct((hidden, dim), F32),
            jax.ShapeDtypeStruct((1, 1), F32),
        ),
        in_specs=[vmem] * 4,
        out_specs=(hbm, hbm, hbm, pl.BlockSpec(memory_space=pltpu.SMEM)),
        scratch_shapes=[sem(3)],
        compiler_params=pltpu.CompilerParams(vmem_limit_bytes=8 << 20),
    )(*[pltpu.with_memory_space_constraint(x, pltpu.VMEM) for x in held])
    return (
        qg.reshape(1, nquery, qlen, dim),
        pg.reshape(1, npass, plen, dim),
        wg,
        loss.reshape(()),
    )


def solution(mesh):
    return jax.shard_map(
        shards,
        mesh=mesh,
        in_specs=(P("rep", "blk", None, None), P("rep", "blk", None, None), P("rep", "blk"), P()),
        out_specs=(P("rep", "blk", None, None), P("rep", "blk", None, None), P(), P()),
        check_vma=False,
    )
```

```python
import functools

import jax
import jax.numpy as jnp
from jax import lax
from jax.experimental import pallas as pl
from jax.experimental.pallas import tpu as pltpu
from jax.sharding import PartitionSpec as P

MESH = pl.DeviceIdType.MESH
F32 = jnp.float32
BF16 = jnp.bfloat16
NT = (((1,), (1,)), ((), ()))
TN = (((0,), (0,)), ((), ()))

temper = 0.5
LANES = 128
LOG2E = 1.4426950408889634
FAR = -1e30


def rows_iota(shape, dim):
    return lax.broadcasted_iota(jnp.int32, shape, dim)


def split_dot(x, ones, terms):
    out = None
    for _ in range(terms):
        part = x.astype(BF16)
        x = x - part.astype(F32)
        dot = jnp.dot(part, ones, preferred_element_type=F32)
        out = dot if out is None else out + dot
    return out


def kernel(
    dims, lens_in, qhid_in, proj_in, phid, qg_out, pg_v, wg_out, loss_out,
    lens, proj, pick, spread, tok, ptok, ptok_t, hid, expo, reach, grads, drawn, tops, sums, sc, lo_c, lo_z, qsend, qrecv,
    wsend, wrecv, zbuf, cbuf,
    in_sem, up, down, tok_s, tok_r, hid_s, hid_r, sc_s, sc_r, lc_s, lc_r, lz_s, lz_r, qg_s, qg_r, ws_s, ws_r,
    z_s, z_r, c_s, c_r,
):
    nblk, nrep, ncore, nquery, qlen, npass, plen = dims
    ntok = nquery * qlen
    nqi = nblk * ntok
    nq_all = nblk * nquery
    ntp = npass * plen
    nfac = npass * nqi
    nz = nrep // ncore
    na = nblk * ncore
    hidden, dim = proj.shape
    total = nq_all * nrep
    parts = wsend.shape[0]
    cols = hidden // parts
    paired = nblk & (nblk - 1) == 0
    blk = lax.axis_index("blk")
    rep = lax.axis_index("rep")
    core = lax.rem(rep, ncore)
    zed = rep // ncore
    me_a = blk * ncore + core

    def mixed(index, k, count):
        if count & (count - 1):
            return lax.rem(index + k, count)
        out = 0
        bit = 1
        while bit < count:
            out = out + lax.rem(index // bit + k // bit, 2) * bit
            bit *= 2
        return out

    def slot_owner(slots):
        return slots ^ blk if paired else lax.rem(blk + nblk - slots, nblk)

    def blk_peer(k):
        return (mixed(blk, k, nblk), rep)

    def core_peer(k):
        return (blk, zed * ncore + lax.rem(core + k, ncore))

    def a_index(k):
        return mixed(me_a, k, na)

    def a_peer(k):
        other = a_index(k)
        return (other // ncore, zed * ncore + lax.rem(other, ncore))

    def z_peer(k):
        return (blk, mixed(zed, k, nz) * ncore + core)

    def z_next(step):
        return (blk, (zed + step) * ncore + core)

    def start_copy(src, dst, send, recv, device):
        copy = pltpu.make_async_remote_copy(
            src_ref=src, dst_ref=dst, send_sem=send, recv_sem=recv, device_id=device, device_id_type=MESH
        )
        copy.start()
        return copy

    def bytes_of(view, send, recv):
        return pltpu.make_async_remote_copy(
            src_ref=view, dst_ref=view, send_sem=send, recv_sem=recv, device_id=a_peer(1), device_id_type=MESH
        )

    def share(src, dst, send, recv, peer, count):
        for k in range(count - 1, 0, -1):
            start_copy(src(k), dst(k), send, recv, peer(k))

    def tell(step):
        @pl.when((zed >= step) & (zed + 1 < nz))
        def _():
            pl.semaphore_signal(up.at[step - 1], inc=1, device_id=z_next(1), device_id_type=MESH)

        @pl.when((zed + step < nz) & (zed >= 1))
        def _():
            pl.semaphore_signal(down.at[step - 1], inc=1, device_id=z_next(-1), device_id_type=MESH)

    def hear(step):
        @pl.when(zed >= step + 1)
        def _():
            pl.semaphore_wait(up.at[step - 1], 1)

        @pl.when(zed + step + 1 < nz)
        def _():
            pl.semaphore_wait(down.at[step - 1], 1)

    barrier = pltpu.get_barrier_semaphore()
    for k in range(na - 1, 0, -1):
        pl.semaphore_signal(barrier, inc=1, device_id=a_peer(k), device_id_type=MESH)

    @pl.when(zed + 1 < nz)
    def _():
        pl.semaphore_signal(barrier, inc=1, device_id=z_next(1), device_id_type=MESH)

    @pl.when(zed >= 1)
    def _():
        pl.semaphore_signal(barrier, inc=1, device_id=z_next(-1), device_id_type=MESH)

    greeted = na - 1 + (zed + nz - 1) // nz + (2 * nz - 2 - zed) // nz

    loads = []
    pairs = [(qhid_in, hid.at[pl.ds(ntp, ntok)]), (proj_in, proj), (lens_in, lens)]
    pairs += [(phid.at[p], hid.at[pl.ds(p * plen, plen)]) for p in range(npass)]
    for n, (src, dst) in enumerate(pairs):
        load = pltpu.make_async_copy(src, dst, in_sem.at[min(n, 3)])
        load.start()
        loads.append(load)
    ppad, qpad = sc.shape[1:]
    token = rows_iota((nqi, qpad), 0)
    query = slot_owner(token // ntok) * nquery + lax.rem(token, ntok) // qlen
    pick[...] = jnp.where(query == rows_iota((nqi, qpad), 1), 1.0, 0.0).astype(BF16)
    token_t = rows_iota((qpad, nqi), 1)
    query_t = slot_owner(token_t // ntok) * nquery + lax.rem(token_t, ntok) // qlen
    spread[...] = jnp.where(query_t == rows_iota((qpad, nqi), 0), 1.0, 0.0).astype(BF16)
    tops[...] = jnp.zeros_like(tops)
    sums[...] = jnp.ones_like(sums)
    unit = jnp.where(rows_iota((ntok, LANES), 1) == 0, 1.0, 0.0).astype(BF16)
    loads[0].wait()
    loads[1].wait()
    tok[0] = jnp.dot(hid[ntp : ntp + ntok, :], proj[...], preferred_element_type=F32).astype(BF16)
    pl.semaphore_wait(barrier, greeted)
    tok_copies = [start_copy(tok.at[0], tok.at[k], tok_s.at[0], tok_r.at[k - 1], blk_peer(k)) for k in range(nblk - 1, 0, -1)][::-1]
    relayed = paired and nblk == 4
    half = ntok // 2

    def send_hid(h, k, slot, source, start, count, recv):
        here = pl.ds(h * cols, cols)
        start_copy(
            hid.at[pl.ds(ntp + source * ntok + start, count), here],
            hid.at[pl.ds(ntp + slot * ntok + start, count), here],
            hid_s.at[0], hid_r.at[recv], blk_peer(k),
        )

    def hid_bytes(h, rows, recv):
        return bytes_of(hid.at[pl.ds(ntp, rows), pl.ds(h * cols, cols)], hid_s.at[0], hid_r.at[recv])

    def relay(h):
        if relayed:
            if h >= 2:
                for k in (1, 2):
                    send_hid(h, k, k, 0, (k + 2) % 2 * half, half, parts + h)
            hid_bytes(h, 2 * half, h).wait_recv()
            send_hid(h, 2, 3, 1, 0, half, parts + h)
            send_hid(h, 1, 3, 2, half, half, parts + h)

    if relayed:
        for turn in range(2):
            for h in range(parts):
                for k in (1, 2):
                    if turn == 0 or h < 2:
                        send_hid(h, k, k, 0, (k + 1 + turn) % 2 * half, half, turn * parts + h)
        late_rows, sent_rows = 4 * half, 6 * half
    else:
        for h in range(parts):
            for k in range(1, nblk):
                send_hid(h, k, k, 0, 0, ntok, parts + h)
        late_rows = sent_rows = (nblk - 1) * ntok
    if nz > 2:
        tell(1)

    loads[2].wait()
    pltpu.make_async_copy(hid.at[pl.ds(0, ntp)], hid.at[pl.ds(0, ntp)], in_sem.at[3]).wait()
    size = jnp.ones((ppad, LANES), jnp.int32)
    for p in range(npass):
        vec = jnp.dot(hid[p * plen : (p + 1) * plen, :], proj[...], preferred_element_type=F32).astype(BF16)
        ptok[p, :, :dim] = vec
        out_of = (rows_iota((plen, LANES), 0) >= lens[0, p]) & (rows_iota((plen, LANES), 1) == 0)
        ptok[p, :, dim:] = jnp.where(out_of, FAR, 0.0).astype(BF16)
        ptok_t[p] = vec.T
        size = jnp.where(rows_iota((ppad, LANES), 0) == p, lens[0, p], size)

    def forward(first, count):
        width = count * ntok
        side = jnp.concatenate([tok[k] for k in range(first, first + count)], 0)
        side = jnp.concatenate([side, jnp.concatenate([unit] * count, 0)], 1)
        here = pl.ds(first * ntok, width)
        for p in range(npass):
            a = lax.dot_general(ptok[p], side, NT, preferred_element_type=F32)
            top = jnp.max(a, 0, keepdims=True)
            e = jnp.exp2((a - top) * (LOG2E / temper))
            expo[p, :, here] = e.astype(BF16)
            tops[pl.ds(p, 1), here] = top
            sums[pl.ds(p, 1), here] = jnp.sum(e, 0, keepdims=True)

    def collect(first, count):
        width = count * ntok
        for p in range(npass):
            m = lax.dot_general(
                expo[p, :, pl.ds(first * ntok, width)], hid[p * plen : (p + 1) * plen, :], TN,
                preferred_element_type=F32,
            )
            drawn[pl.ds(p * nqi + first * ntok, width), :] = m.astype(BF16)

    forward(0, 1)
    collect(0, 1)
    for k in range(1, nblk - 1):
        tok_copies[k - 1].wait_recv()
    if nblk > 2:
        forward(1, nblk - 2)
    if nblk > 1:
        tok_copies[nblk - 2].wait_recv()
        forward(nblk - 1, 1)

    log_size = jnp.log(size.astype(F32))[:, :1]
    pooled = temper * (tops[...] * (1.0 / temper) + jnp.log(sums[...]) - log_size)
    own = split_dot(pooled, pick[...], 3)
    sc[0] = own
    share(lambda k: sc.at[0], lambda k: sc.at[k], sc_s.at[0], sc_r.at[0], blk_peer, nblk)
    sc_all = bytes_of(sc.at[pl.ds(0, nblk - 1)], sc_s.at[0], sc_r.at[0])
    inv = 1.0 / sums[...]
    every_t = jnp.concatenate([tok[k].astype(F32).T for k in range(nblk)], 1)
    relay(0)
    later = list(range(1, parts))
    for p in range(npass):
        reach[p] = jnp.dot(ptok_t[p], expo[p], preferred_element_type=F32)
        if later and p % 2 == 0:
            relay(later.pop(0))
    for h in later:
        relay(h)
    if nblk > 1:
        collect(1, nblk - 1)
    if nz > 2:
        for step in range(1, nz - 1):
            hear(step)
            if step + 1 < nz - 1:
                tell(step + 1)
    if nblk > 1:
        sc_all.wait_recv()

    score = sc[...]
    row = rows_iota(score.shape, 1)
    lane = rows_iota(score.shape, 2)
    slot = rows_iota(score.shape, 0)
    live = row < npass
    hidden_score = jnp.where(live, score, -jnp.inf)
    top = jnp.max(jnp.max(hidden_score, 0), 0, keepdims=True)
    lse = top + jnp.log(jnp.sum(jnp.sum(jnp.exp(hidden_score - top[None]), 0), 0, keepdims=True))
    mine = rows_iota(own.shape, 0) + blk * npass == rows_iota(own.shape, 1)
    dscore = (jnp.exp(sc[0] - lse) - mine.astype(F32)) / total
    factor = split_dot(dscore, spread[...], 3) * inv

    for p in range(npass):
        grads[:, p * nqi : (p + 1) * nqi] = (every_t * factor[p : p + 1]).astype(BF16)
    qg_t = reach[0] * factor[0:1]
    for p in range(1, npass):
        qg_t = qg_t + reach[p] * factor[p : p + 1]
    qg_b = qg_t.astype(BF16)
    grads[:, nfac:] = qg_b
    for k in range(1, nblk):
        qsend[k] = qg_b[:, k * ntok : (k + 1) * ntok]

    for h in range(parts):
        here = slice(h * cols, (h + 1) * cols)
        w = jnp.dot(grads[:, :nfac], drawn[:, here], preferred_element_type=F32)
        if nblk > 1:
            hid_bytes(h, late_rows, parts + h).wait_recv()
        w = w + jnp.dot(grads[:, nfac:], hid[ntp:, here], preferred_element_type=F32)
        w = w.T.astype(BF16).reshape(na, cols // na, dim)
        wsend[h] = w
        wrecv[h, me_a] = wsend[h, me_a]
        share(lambda k: wsend.at[h, a_index(k)], lambda k: wrecv.at[h, me_a], ws_s.at[0], ws_r.at[h], a_peer, na)

    share(lambda k: qsend.at[k], lambda k: qrecv.at[k], qg_s.at[0], qg_r.at[0], blk_peer, nblk)
    qg_all = bytes_of(qrecv.at[pl.ds(0, nblk - 1)], qg_s.at[0], qg_r.at[0])

    hit = live & (slot_owner(slot) * npass + row == lane)
    aim = jnp.sum(jnp.sum(jnp.where(hit, score, 0.0), 0), 0, keepdims=True)
    gap = jnp.where(rows_iota(lse.shape, 1) < nq_all, lse - aim, 0.0)
    lo_c[core] = jnp.broadcast_to(jnp.sum(gap, 1, keepdims=True), lo_c.shape[1:])
    share(lambda k: lo_c.at[core], lambda k: lo_c.at[core], lc_s.at[0], lc_r.at[0], core_peer, ncore)
    lc_all = bytes_of(lo_c.at[pl.ds(0, ncore - 1)], lc_s.at[0], lc_r.at[0])
    for p in range(npass):
        pg_v[p] = lax.dot_general(
            expo[p], grads[:, p * nqi : (p + 1) * nqi], NT, preferred_element_type=F32
        )
    if ncore > 1:
        lc_all.wait_recv()
    lo_z[zed] = jnp.sum(lo_c[...], 0)
    share(lambda k: lo_z.at[zed], lambda k: lo_z.at[zed], lz_s.at[0], lz_r.at[0], z_peer, nz)
    lz_all = bytes_of(lo_z.at[pl.ds(0, nz - 1)], lz_s.at[0], lz_r.at[0])
    for h in range(parts):
        if na > 1:
            bytes_of(wrecv.at[h, pl.ds(0, na - 1)], ws_s.at[0], ws_r.at[h]).wait_recv()
        zbuf[h, zed] = jnp.sum(wrecv[h].astype(F32), 0).astype(BF16)
        share(lambda k: zbuf.at[h, zed], lambda k: zbuf.at[h, zed], z_s.at[0], z_r.at[h], z_peer, nz)
    if nblk > 1:
        qg_all.wait_recv()
    mine_t = grads[:, nfac : nfac + ntok].astype(F32)
    for k in range(1, nblk):
        mine_t = mine_t + qrecv[k].astype(F32)
    qg_out[...] = mine_t.T
    if nz > 1:
        lz_all.wait_recv()
    loss_out[...] = jnp.sum(lo_z[...], 0) / total
    for h in range(parts):
        if nz > 1:
            bytes_of(zbuf.at[h, pl.ds(0, nz - 1)], z_s.at[0], z_r.at[h]).wait_recv()
        cbuf[h, me_a] = jnp.sum(zbuf[h].astype(F32), 0).astype(BF16)
        share(lambda k: cbuf.at[h, me_a], lambda k: cbuf.at[h, me_a], c_s.at[0], c_r.at[h], a_peer, na)
    if nblk > 1:
        bytes_of(tok.at[pl.ds(1, nblk - 1)], tok_s.at[0], tok_r.at[0]).wait_send()
        bytes_of(hid.at[pl.ds(ntp, sent_rows)], hid_s.at[0], hid_r.at[0]).wait_send()
        sc_all.wait_send()
        qg_all.wait_send()
    if ncore > 1:
        lc_all.wait_send()
    if na > 1:
        bytes_of(wsend.at[:, pl.ds(0, na - 1)], ws_s.at[0], ws_r.at[0]).wait_send()
    if nz > 1:
        lz_all.wait_send()
        bytes_of(zbuf.at[:, pl.ds(0, nz - 1)], z_s.at[0], z_r.at[0]).wait_send()
    for h in range(parts):
        if na > 1:
            bytes_of(cbuf.at[h, pl.ds(0, na - 1)], c_s.at[0], c_r.at[h]).wait_recv()
        wg_out[h * cols : (h + 1) * cols, :] = cbuf[h].astype(F32).reshape(cols, dim)
    if na > 1:
        bytes_of(cbuf.at[:, pl.ds(0, na - 1)], c_s.at[0], c_r.at[0]).wait_send()


def write_out(qg, pg, wg, loss, qg_out, pg_out, wg_out, loss_out, held, sem):
    held[0, 0] = loss[0, 0]
    copies = []
    for n, (src, dst) in enumerate(((pg, pg_out), (wg, wg_out), (qg, qg_out), (held, loss_out))):
        copy = pltpu.make_async_copy(src, dst, sem.at[n])
        copy.start()
        copies.append(copy)
    for copy in copies:
        copy.wait()


def shards(query_hidden, passage_hidden, lengths, projection):
    hidden, dim = projection.shape
    nquery, qlen = query_hidden.shape[1:3]
    npass, plen = passage_hidden.shape[1:3]
    nblk = lax.axis_size("blk")
    nrep = lax.axis_size("rep")
    ncore = 2 if nrep % 2 == 0 else 1
    nz = nrep // ncore
    na = nblk * ncore
    ntok = nquery * qlen
    nqi = nblk * ntok
    ntp = npass * plen
    ppad = -(-npass // 8) * 8
    qpad = -(-nblk * nquery // LANES) * LANES
    parts = 3 if hidden % (3 * 16 * na) == 0 else 1
    deep = hidden // parts // na
    dims = (nblk, nrep, ncore, nquery, qlen, npass, plen)
    vmem = pl.BlockSpec(memory_space=pltpu.VMEM)
    sem = lambda *n: pltpu.SemaphoreType.DMA(tuple(max(i, 1) for i in n))
    flag = pltpu.SemaphoreType.REGULAR((max(nz - 2, 1),))
    pairs = [sem(1), sem(nblk - 1), sem(1), sem(2 * parts)]
    pairs += [sem(1)] * 8
    pairs += [sem(1), sem(parts)] * 3
    held = pl.pallas_call(
        functools.partial(kernel, dims),
        out_shape=(
            pltpu.VMEM((ntok, dim), F32),
            pltpu.VMEM((npass, plen, dim), F32),
            pltpu.VMEM((hidden, dim), F32),
            pltpu.VMEM((8, LANES), F32),
        ),
        in_specs=[
            *[pl.BlockSpec(memory_space=pl.ANY)] * 4,
        ],
        out_specs=(vmem, vmem, vmem, vmem),
        scratch_shapes=[
            pltpu.SMEM((1, npass), jnp.int32),
            pltpu.VMEM((hidden, dim), BF16),
            pltpu.VMEM((nqi, qpad), BF16),
            pltpu.VMEM((qpad, nqi), BF16),
            pltpu.VMEM((nblk, ntok, dim), BF16),
            pltpu.VMEM((npass, plen, dim + LANES), BF16),
            pltpu.VMEM((npass, dim, plen), BF16),
            pltpu.VMEM((ntp + nqi, hidden), BF16),
            pltpu.VMEM((npass, plen, nqi), BF16),
            pltpu.VMEM((npass, dim, nqi), F32),
            pltpu.VMEM((dim, npass * nqi + nqi), BF16),
            pltpu.VMEM((npass * nqi, hidden), BF16),
            pltpu.VMEM((ppad, nqi), F32),
            pltpu.VMEM((ppad, nqi), F32),
            pltpu.VMEM((nblk, ppad, qpad), F32),
            pltpu.VMEM((ncore, 8, LANES), F32),
            pltpu.VMEM((nz, 8, LANES), F32),
            pltpu.VMEM((nblk, dim, ntok), BF16),
            pltpu.VMEM((nblk, dim, ntok), BF16),
            pltpu.VMEM((parts, na, deep, dim), BF16),
            pltpu.VMEM((parts, na, deep, dim), BF16),
            pltpu.VMEM((parts, nz, deep, dim), BF16),
            pltpu.VMEM((parts, na, deep, dim), BF16),
            sem(4),
            flag,
            flag,
        ] + pairs,
        compiler_params=pltpu.CompilerParams(
            collective_id=0, has_side_effects=True, vmem_limit_bytes=56 << 20
        ),
    )(
        lengths,
        query_hidden.reshape(ntok, hidden),
        projection,
        passage_hidden.reshape(npass, plen, hidden),
    )
    hbm = pl.BlockSpec(memory_space=pl.ANY)
    qg, pg, wg, loss = pl.pallas_call(
        write_out,
        out_shape=(
            jax.ShapeDtypeStruct((ntok, dim), F32),
            jax.ShapeDtypeStruct((npass, plen, dim), F32),
            jax.ShapeDtypeStruct((hidden, dim), F32),
            jax.ShapeDtypeStruct((1, 1), F32),
        ),
        in_specs=[vmem] * 4,
        out_specs=(hbm, hbm, hbm, hbm),
        scratch_shapes=[pltpu.SMEM((1, 1), F32), sem(4)],
        compiler_params=pltpu.CompilerParams(vmem_limit_bytes=8 << 20),
    )(*[pltpu.with_memory_space_constraint(x, pltpu.VMEM) for x in held])
    return (
        qg.reshape(1, nquery, qlen, dim),
        pg.reshape(1, npass, plen, dim),
        wg,
        loss.reshape(()),
    )


def solution(mesh):
    return jax.shard_map(
        shards,
        mesh=mesh,
        in_specs=(P("rep", "blk", None, None), P("rep", "blk", None, None), P("rep", "blk"), P()),
        out_specs=(P("rep", "blk", None, None), P("rep", "blk", None, None), P(), P()),
        check_vma=False,
    )
```

```python
import functools

import jax
import jax.numpy as jnp
from jax import lax
from jax.experimental import pallas as pl
from jax.experimental.pallas import tpu as pltpu
from jax.sharding import PartitionSpec as P

MESH = pl.DeviceIdType.MESH
F32 = jnp.float32
BF16 = jnp.bfloat16
NT = (((1,), (1,)), ((), ()))
TN = (((0,), (0,)), ((), ()))

temper = 0.5
LANES = 128
LOG2E = 1.4426950408889634
FAR = -1e30


def rows_iota(shape, dim):
    return lax.broadcasted_iota(jnp.int32, shape, dim)


def split_dot(x, ones, terms):
    out = None
    for _ in range(terms):
        part = x.astype(BF16)
        x = x - part.astype(F32)
        dot = jnp.dot(part, ones, preferred_element_type=F32)
        out = dot if out is None else out + dot
    return out


def kernel(
    dims, lens_in, qhid_in, proj_in, phid, qg_out, pg_v, wg_out, loss_out,
    lens, proj, pick, spread, tok, ptok, ptok_t, hid, expo, reach, grads, drawn, tops, sums, sc, lo_c, lo_z, qsend, qrecv,
    wsend, wrecv, zbuf, cbuf,
    in_sem, up, down, tok_s, tok_r, hid_s, hid_r, sc_s, sc_r, lc_s, lc_r, lz_s, lz_r, qg_s, qg_r, ws_s, ws_r,
    z_s, z_r, c_s, c_r,
):
    nblk, nrep, ncore, nquery, qlen, npass, plen = dims
    ntok = nquery * qlen
    nqi = nblk * ntok
    nq_all = nblk * nquery
    ntp = npass * plen
    nfac = npass * nqi
    nz = nrep // ncore
    na = nblk * ncore
    hidden, dim = proj.shape
    total = nq_all * nrep
    parts = wsend.shape[0]
    cols = hidden // parts
    paired = nblk & (nblk - 1) == 0
    blk = lax.axis_index("blk")
    rep = lax.axis_index("rep")
    core = lax.rem(rep, ncore)
    zed = rep // ncore
    me_a = blk * ncore + core

    def mixed(index, k, count):
        if count & (count - 1):
            return lax.rem(index + k, count)
        out = 0
        bit = 1
        while bit < count:
            out = out + lax.rem(index // bit + k // bit, 2) * bit
            bit *= 2
        return out

    def slot_owner(slots):
        return slots ^ blk if paired else lax.rem(blk + nblk - slots, nblk)

    def blk_peer(k):
        return (mixed(blk, k, nblk), rep)

    def core_peer(k):
        return (blk, zed * ncore + lax.rem(core + k, ncore))

    def a_index(k):
        return mixed(me_a, k, na)

    def a_peer(k):
        other = a_index(k)
        return (other // ncore, zed * ncore + lax.rem(other, ncore))

    def z_peer(k):
        return (blk, mixed(zed, k, nz) * ncore + core)

    def z_next(step):
        return (blk, (zed + step) * ncore + core)

    def start_copy(src, dst, send, recv, device):
        copy = pltpu.make_async_remote_copy(
            src_ref=src, dst_ref=dst, send_sem=send, recv_sem=recv, device_id=device, device_id_type=MESH
        )
        copy.start()
        return copy

    def bytes_of(view, send, recv):
        return pltpu.make_async_remote_copy(
            src_ref=view, dst_ref=view, send_sem=send, recv_sem=recv, device_id=a_peer(1), device_id_type=MESH
        )

    def share(src, dst, send, recv, peer, count):
        for k in range(count - 1, 0, -1):
            start_copy(src(k), dst(k), send, recv, peer(k))

    def tell(step):
        @pl.when((zed >= step) & (zed + 1 < nz))
        def _():
            pl.semaphore_signal(up.at[step - 1], inc=1, device_id=z_next(1), device_id_type=MESH)

        @pl.when((zed + step < nz) & (zed >= 1))
        def _():
            pl.semaphore_signal(down.at[step - 1], inc=1, device_id=z_next(-1), device_id_type=MESH)

    def hear(step):
        @pl.when(zed >= step + 1)
        def _():
            pl.semaphore_wait(up.at[step - 1], 1)

        @pl.when(zed + step + 1 < nz)
        def _():
            pl.semaphore_wait(down.at[step - 1], 1)

    barrier = pltpu.get_barrier_semaphore()
    for k in range(na - 1, 0, -1):
        pl.semaphore_signal(barrier, inc=1, device_id=a_peer(k), device_id_type=MESH)

    @pl.when(zed + 1 < nz)
    def _():
        pl.semaphore_signal(barrier, inc=1, device_id=z_next(1), device_id_type=MESH)

    @pl.when(zed >= 1)
    def _():
        pl.semaphore_signal(barrier, inc=1, device_id=z_next(-1), device_id_type=MESH)

    greeted = na - 1 + (zed + nz - 1) // nz + (2 * nz - 2 - zed) // nz

    loads = []
    pairs = [(qhid_in, hid.at[pl.ds(ntp, ntok)]), (proj_in, proj), (lens_in, lens)]
    pairs += [(phid.at[p], hid.at[pl.ds(p * plen, plen)]) for p in range(npass)]
    for n, (src, dst) in enumerate(pairs):
        load = pltpu.make_async_copy(src, dst, in_sem.at[min(n, 3)])
        load.start()
        loads.append(load)
    ppad, qpad = sc.shape[1:]
    token = rows_iota((nqi, qpad), 0)
    query = slot_owner(token // ntok) * nquery + lax.rem(token, ntok) // qlen
    pick[...] = jnp.where(query == rows_iota((nqi, qpad), 1), 1.0, 0.0).astype(BF16)
    token_t = rows_iota((qpad, nqi), 1)
    query_t = slot_owner(token_t // ntok) * nquery + lax.rem(token_t, ntok) // qlen
    spread[...] = jnp.where(query_t == rows_iota((qpad, nqi), 0), 1.0, 0.0).astype(BF16)
    tops[...] = jnp.zeros_like(tops)
    sums[...] = jnp.ones_like(sums)
    unit = jnp.where(rows_iota((ntok, LANES), 1) == 0, 1.0, 0.0).astype(BF16)
    loads[0].wait()
    loads[1].wait()
    tok[0] = jnp.dot(hid[ntp : ntp + ntok, :], proj[...], preferred_element_type=F32).astype(BF16)
    pl.semaphore_wait(barrier, greeted)
    tok_copies = [start_copy(tok.at[0], tok.at[k], tok_s.at[0], tok_r.at[k - 1], blk_peer(k)) for k in range(nblk - 1, 0, -1)][::-1]
    relayed = paired and nblk == 4
    half = ntok // 2

    def send_hid(h, k, slot, source, start, count, recv):
        here = pl.ds(h * cols, cols)
        start_copy(
            hid.at[pl.ds(ntp + source * ntok + start, count), here],
            hid.at[pl.ds(ntp + slot * ntok + start, count), here],
            hid_s.at[0], hid_r.at[recv], blk_peer(k),
        )

    def hid_bytes(h, rows, recv):
        return bytes_of(hid.at[pl.ds(ntp, rows), pl.ds(h * cols, cols)], hid_s.at[0], hid_r.at[recv])

    def relay(h):
        if relayed:
            if h >= 2:
                for k in (1, 2):
                    send_hid(h, k, k, 0, (k + 2) % 2 * half, half, parts + h)
            hid_bytes(h, 2 * half, h).wait_recv()
            send_hid(h, 2, 3, 1, 0, half, parts + h)
            send_hid(h, 1, 3, 2, half, half, parts + h)

    if relayed:
        late_rows, sent_rows = 4 * half, 6 * half
    else:
        for h in range(parts):
            for k in range(1, nblk):
                send_hid(h, k, k, 0, 0, ntok, parts + h)
        late_rows = sent_rows = (nblk - 1) * ntok
    if nz > 2:
        tell(1)

    loads[2].wait()
    pltpu.make_async_copy(hid.at[pl.ds(0, ntp)], hid.at[pl.ds(0, ntp)], in_sem.at[3]).wait()
    size = jnp.ones((ppad, LANES), jnp.int32)
    for p in range(npass):
        vec = jnp.dot(hid[p * plen : (p + 1) * plen, :], proj[...], preferred_element_type=F32).astype(BF16)
        ptok[p, :, :dim] = vec
        out_of = (rows_iota((plen, LANES), 0) >= lens[0, p]) & (rows_iota((plen, LANES), 1) == 0)
        ptok[p, :, dim:] = jnp.where(out_of, FAR, 0.0).astype(BF16)
        ptok_t[p] = vec.T
        size = jnp.where(rows_iota((ppad, LANES), 0) == p, lens[0, p], size)
        if relayed and p == 0:
            for turn in range(2):
                for h in range(parts):
                    for k in (1, 2):
                        if turn == 0 or h < 2:
                            send_hid(h, k, k, 0, (k + 1 + turn) % 2 * half, half, turn * parts + h)

    def forward(first, count):
        width = count * ntok
        side = jnp.concatenate([tok[k] for k in range(first, first + count)], 0)
        side = jnp.concatenate([side, jnp.concatenate([unit] * count, 0)], 1)
        here = pl.ds(first * ntok, width)
        for p in range(npass):
            a = lax.dot_general(ptok[p], side, NT, preferred_element_type=F32)
            top = jnp.max(a, 0, keepdims=True)
            e = jnp.exp2((a - top) * (LOG2E / temper))
            expo[p, :, here] = e.astype(BF16)
            tops[pl.ds(p, 1), here] = top
            sums[pl.ds(p, 1), here] = jnp.sum(e, 0, keepdims=True)

    def collect(first, count):
        width = count * ntok
        for p in range(npass):
            m = lax.dot_general(
                expo[p, :, pl.ds(first * ntok, width)], hid[p * plen : (p + 1) * plen, :], TN,
                preferred_element_type=F32,
            )
            drawn[pl.ds(p * nqi + first * ntok, width), :] = m.astype(BF16)

    forward(0, 1)
    collect(0, 1)
    for k in range(1, nblk - 1):
        tok_copies[k - 1].wait_recv()
    if nblk > 2:
        forward(1, nblk - 2)
    if nblk > 1:
        tok_copies[nblk - 2].wait_recv()
        forward(nblk - 1, 1)

    log_size = jnp.log(size.astype(F32))[:, :1]
    pooled = temper * (tops[...] * (1.0 / temper) + jnp.log(sums[...]) - log_size)
    own = split_dot(pooled, pick[...], 3)
    sc[0] = own
    share(lambda k: sc.at[0], lambda k: sc.at[k], sc_s.at[0], sc_r.at[0], blk_peer, nblk)
    sc_all = bytes_of(sc.at[pl.ds(0, nblk - 1)], sc_s.at[0], sc_r.at[0])
    inv = 1.0 / sums[...]
    every_t = jnp.concatenate([tok[k].astype(F32).T for k in range(nblk)], 1)
    relay(0)
    later = list(range(1, parts))
    for p in range(npass):
        reach[p] = jnp.dot(ptok_t[p], expo[p], preferred_element_type=F32)
        if later and p % 2 == 0:
            relay(later.pop(0))
    for h in later:
        relay(h)
    if nblk > 1:
        collect(1, nblk - 1)
    if nz > 2:
        for step in range(1, nz - 1):
            hear(step)
            if step + 1 < nz - 1:
                tell(step + 1)
    if nblk > 1:
        sc_all.wait_recv()

    score = sc[...]
    row = rows_iota(score.shape, 1)
    lane = rows_iota(score.shape, 2)
    slot = rows_iota(score.shape, 0)
    live = row < npass
    hidden_score = jnp.where(live, score, -jnp.inf)
    top = jnp.max(jnp.max(hidden_score, 0), 0, keepdims=True)
    lse = top + jnp.log(jnp.sum(jnp.sum(jnp.exp(hidden_score - top[None]), 0), 0, keepdims=True))
    mine = rows_iota(own.shape, 0) + blk * npass == rows_iota(own.shape, 1)
    dscore = (jnp.exp(sc[0] - lse) - mine.astype(F32)) / total
    factor = split_dot(dscore, spread[...], 3) * inv

    for p in range(npass):
        grads[:, p * nqi : (p + 1) * nqi] = (every_t * factor[p : p + 1]).astype(BF16)
    qg_t = reach[0] * factor[0:1]
    for p in range(1, npass):
        qg_t = qg_t + reach[p] * factor[p : p + 1]
    qg_b = qg_t.astype(BF16)
    grads[:, nfac:] = qg_b
    for k in range(1, nblk):
        qsend[k] = qg_b[:, k * ntok : (k + 1) * ntok]

    for h in range(parts):
        here = slice(h * cols, (h + 1) * cols)
        w = jnp.dot(grads[:, :nfac], drawn[:, here], preferred_element_type=F32)
        if nblk > 1:
            hid_bytes(h, late_rows, parts + h).wait_recv()
        w = w + jnp.dot(grads[:, nfac:], hid[ntp:, here], preferred_element_type=F32)
        w = w.T.astype(BF16).reshape(na, cols // na, dim)
        wsend[h] = w
        wrecv[h, me_a] = wsend[h, me_a]
        share(lambda k: wsend.at[h, a_index(k)], lambda k: wrecv.at[h, me_a], ws_s.at[0], ws_r.at[h], a_peer, na)

    share(lambda k: qsend.at[k], lambda k: qrecv.at[k], qg_s.at[0], qg_r.at[0], blk_peer, nblk)
    qg_all = bytes_of(qrecv.at[pl.ds(0, nblk - 1)], qg_s.at[0], qg_r.at[0])

    hit = live & (slot_owner(slot) * npass + row == lane)
    aim = jnp.sum(jnp.sum(jnp.where(hit, score, 0.0), 0), 0, keepdims=True)
    gap = jnp.where(rows_iota(lse.shape, 1) < nq_all, lse - aim, 0.0)
    lo_c[core] = jnp.broadcast_to(jnp.sum(gap, 1, keepdims=True), lo_c.shape[1:])
    share(lambda k: lo_c.at[core], lambda k: lo_c.at[core], lc_s.at[0], lc_r.at[0], core_peer, ncore)
    lc_all = bytes_of(lo_c.at[pl.ds(0, ncore - 1)], lc_s.at[0], lc_r.at[0])
    for p in range(npass):
        pg_v[p] = lax.dot_general(
            expo[p], grads[:, p * nqi : (p + 1) * nqi], NT, preferred_element_type=F32
        )
    if ncore > 1:
        lc_all.wait_recv()
    lo_z[zed] = jnp.sum(lo_c[...], 0)
    share(lambda k: lo_z.at[zed], lambda k: lo_z.at[zed], lz_s.at[0], lz_r.at[0], z_peer, nz)
    lz_all = bytes_of(lo_z.at[pl.ds(0, nz - 1)], lz_s.at[0], lz_r.at[0])
    for h in range(parts):
        if na > 1:
            bytes_of(wrecv.at[h, pl.ds(0, na - 1)], ws_s.at[0], ws_r.at[h]).wait_recv()
        zbuf[h, zed] = jnp.sum(wrecv[h].astype(F32), 0).astype(BF16)
        share(lambda k: zbuf.at[h, zed], lambda k: zbuf.at[h, zed], z_s.at[0], z_r.at[h], z_peer, nz)
    if nblk > 1:
        qg_all.wait_recv()
    mine_t = grads[:, nfac : nfac + ntok].astype(F32)
    for k in range(1, nblk):
        mine_t = mine_t + qrecv[k].astype(F32)
    qg_out[...] = mine_t.T
    if nz > 1:
        lz_all.wait_recv()
    loss_out[...] = jnp.sum(lo_z[...], 0) / total
    for h in range(parts):
        if nz > 1:
            bytes_of(zbuf.at[h, pl.ds(0, nz - 1)], z_s.at[0], z_r.at[h]).wait_recv()
        cbuf[h, me_a] = jnp.sum(zbuf[h].astype(F32), 0).astype(BF16)
        share(lambda k: cbuf.at[h, me_a], lambda k: cbuf.at[h, me_a], c_s.at[0], c_r.at[h], a_peer, na)
    if nblk > 1:
        bytes_of(tok.at[pl.ds(1, nblk - 1)], tok_s.at[0], tok_r.at[0]).wait_send()
        bytes_of(hid.at[pl.ds(ntp, sent_rows)], hid_s.at[0], hid_r.at[0]).wait_send()
        sc_all.wait_send()
        qg_all.wait_send()
    if ncore > 1:
        lc_all.wait_send()
    if na > 1:
        bytes_of(wsend.at[:, pl.ds(0, na - 1)], ws_s.at[0], ws_r.at[0]).wait_send()
    if nz > 1:
        lz_all.wait_send()
        bytes_of(zbuf.at[:, pl.ds(0, nz - 1)], z_s.at[0], z_r.at[0]).wait_send()
    for h in range(parts):
        if na > 1:
            bytes_of(cbuf.at[h, pl.ds(0, na - 1)], c_s.at[0], c_r.at[h]).wait_recv()
        wg_out[h * cols : (h + 1) * cols, :] = cbuf[h].astype(F32).reshape(cols, dim)
    if na > 1:
        bytes_of(cbuf.at[:, pl.ds(0, na - 1)], c_s.at[0], c_r.at[0]).wait_send()


def write_out(qg, pg, wg, loss, qg_out, pg_out, wg_out, loss_out, held, sem):
    copies = []
    for n, (src, dst) in enumerate(((pg, pg_out), (wg, wg_out), (qg, qg_out), (held, loss_out))):
        if n == 3:
            held[0, 0] = loss[0, 0]
        copy = pltpu.make_async_copy(src, dst, sem.at[n])
        copy.start()
        copies.append(copy)
    for copy in copies:
        copy.wait()


def shards(query_hidden, passage_hidden, lengths, projection):
    hidden, dim = projection.shape
    nquery, qlen = query_hidden.shape[1:3]
    npass, plen = passage_hidden.shape[1:3]
    nblk = lax.axis_size("blk")
    nrep = lax.axis_size("rep")
    ncore = 2 if nrep % 2 == 0 else 1
    nz = nrep // ncore
    na = nblk * ncore
    ntok = nquery * qlen
    nqi = nblk * ntok
    ntp = npass * plen
    ppad = -(-npass // 8) * 8
    qpad = -(-nblk * nquery // LANES) * LANES
    parts = 3 if hidden % (3 * 16 * na) == 0 else 1
    deep = hidden // parts // na
    dims = (nblk, nrep, ncore, nquery, qlen, npass, plen)
    vmem = pl.BlockSpec(memory_space=pltpu.VMEM)
    sem = lambda *n: pltpu.SemaphoreType.DMA(tuple(max(i, 1) for i in n))
    flag = pltpu.SemaphoreType.REGULAR((max(nz - 2, 1),))
    pairs = [sem(1), sem(nblk - 1), sem(1), sem(2 * parts)]
    pairs += [sem(1)] * 8
    pairs += [sem(1), sem(parts)] * 3
    held = pl.pallas_call(
        functools.partial(kernel, dims),
        out_shape=(
            pltpu.VMEM((ntok, dim), F32),
            pltpu.VMEM((npass, plen, dim), F32),
            pltpu.VMEM((hidden, dim), F32),
            pltpu.VMEM((8, LANES), F32),
        ),
        in_specs=[
            *[pl.BlockSpec(memory_space=pl.ANY)] * 4,
        ],
        out_specs=(vmem, vmem, vmem, vmem),
        scratch_shapes=[
            pltpu.SMEM((1, npass), jnp.int32),
            pltpu.VMEM((hidden, dim), BF16),
            pltpu.VMEM((nqi, qpad), BF16),
            pltpu.VMEM((qpad, nqi), BF16),
            pltpu.VMEM((nblk, ntok, dim), BF16),
            pltpu.VMEM((npass, plen, dim + LANES), BF16),
            pltpu.VMEM((npass, dim, plen), BF16),
            pltpu.VMEM((ntp + nqi, hidden), BF16),
            pltpu.VMEM((npass, plen, nqi), BF16),
            pltpu.VMEM((npass, dim, nqi), F32),
            pltpu.VMEM((dim, npass * nqi + nqi), BF16),
            pltpu.VMEM((npass * nqi, hidden), BF16),
            pltpu.VMEM((ppad, nqi), F32),
            pltpu.VMEM((ppad, nqi), F32),
            pltpu.VMEM((nblk, ppad, qpad), F32),
            pltpu.VMEM((ncore, 8, LANES), F32),
            pltpu.VMEM((nz, 8, LANES), F32),
            pltpu.VMEM((nblk, dim, ntok), BF16),
            pltpu.VMEM((nblk, dim, ntok), BF16),
            pltpu.VMEM((parts, na, deep, dim), BF16),
            pltpu.VMEM((parts, na, deep, dim), BF16),
            pltpu.VMEM((parts, nz, deep, dim), BF16),
            pltpu.VMEM((parts, na, deep, dim), BF16),
            sem(4),
            flag,
            flag,
        ] + pairs,
        compiler_params=pltpu.CompilerParams(
            collective_id=0, has_side_effects=True, vmem_limit_bytes=56 << 20
        ),
    )(
        lengths,
        query_hidden.reshape(ntok, hidden),
        projection,
        passage_hidden.reshape(npass, plen, hidden),
    )
    hbm = pl.BlockSpec(memory_space=pl.ANY)
    qg, pg, wg, loss = pl.pallas_call(
        write_out,
        out_shape=(
            jax.ShapeDtypeStruct((ntok, dim), F32),
            jax.ShapeDtypeStruct((npass, plen, dim), F32),
            jax.ShapeDtypeStruct((hidden, dim), F32),
            jax.ShapeDtypeStruct((1, 1), F32),
        ),
        in_specs=[vmem] * 4,
        out_specs=(hbm, hbm, hbm, hbm),
        scratch_shapes=[pltpu.SMEM((1, 1), F32), sem(4)],
        compiler_params=pltpu.CompilerParams(vmem_limit_bytes=8 << 20),
    )(*[pltpu.with_memory_space_constraint(x, pltpu.VMEM) for x in held])
    return (
        qg.reshape(1, nquery, qlen, dim),
        pg.reshape(1, npass, plen, dim),
        wg,
        loss.reshape(()),
    )


def solution(mesh):
    return jax.shard_map(
        shards,
        mesh=mesh,
        in_specs=(P("rep", "blk", None, None), P("rep", "blk", None, None), P("rep", "blk"), P()),
        out_specs=(P("rep", "blk", None, None), P("rep", "blk", None, None), P(), P()),
        check_vma=False,
    )
```
